128 devices in a mesh: bucket: 8 (over y, core), member: 16 (over z, x).
Axes of the slice: x: 4, y: 4, z: 4, core: 2. Of those that a mesh axis runs over, the one named last changes fastest.
Arguments:
- loader_rows: float32 [8192, 4096], P(('bucket', 'member')), may hold values from -12 to 12
- dest_bucket: int32 [8192], P(('bucket', 'member')), may hold values from 0 to 7, as said below
- dest_slot: int32 [8192], P(('bucket', 'member')), may hold values from 0 to 127, as said below
- noise: float32 [32768, 4096], P(('bucket', 'member')), may hold values from -12 to 12
Outputs:
- targets: float32 [32768, 4096], P(('bucket', 'member'))
The draws below stay inside these ranges and needn't reach their ends.
Inputs may be any that keep to these rules, and one draw needn't show every extreme that they name: Loaded row r goes to bucket group dest_bucket[r] on the device of that group with the same member index as its loader device. No loader device sends more than 16 rows to one bucket group; on every member index one bucket group receives exactly 16 rows from every loader device, and every bucket group is so filled on some member index. `dest_slot`: rows that reach the same device have distinct slots.
All inputs are finite; a program needn't handle non-finite values.
Results may differ from the reference program's by a relative error of at most 0.012.
The reference program's roundings to bfloat16 on the way count: a program that leaves them out, or rounds other values in their place, can miss the bound.
Values may be sent and summed in bfloat16 or wider, within the bound.
A program may use at most 128 MiB of HBM per device.

```python
import math
import jax
import jax.numpy as jnp
from jax import lax

D = 4096
ROWS_DEV = 128
ITERS = 4
BUCKETS = 8
MEMBERS = 16
LOAD_DEV = 64
LOAD_TOTAL = 8192
ROWS_TOTAL = 2048
NOISE_TOTAL = 4096


def routing(key):
    capacity = ROWS_DEV // BUCKETS
    base_key = jax.random.fold_in(key, 41)
    hot_order = jax.random.permutation(jax.random.fold_in(base_key, 1), BUCKETS).astype(jnp.int32)
    senders = jnp.arange(BUCKETS * MEMBERS, dtype=jnp.int32)

    def one_sender(sender):
        sender_key = jax.random.fold_in(jax.random.fold_in(base_key, 2), sender)
        hot_bucket = hot_order[sender % MEMBERS % BUCKETS]
        chosen = jax.random.permutation(jax.random.fold_in(sender_key, 1), (BUCKETS - 1) * capacity)[:LOAD_DEV - capacity]
        others = (chosen // capacity).astype(jnp.int32)
        others = others + (others >= hot_bucket).astype(jnp.int32)
        listing = jnp.concatenate([jnp.full((capacity,), hot_bucket, jnp.int32), others])
        return listing[jax.random.permutation(jax.random.fold_in(sender_key, 2), LOAD_DEV)]
    destination = jax.vmap(one_sender)(senders)
    hits = (destination[:, :, None] == jnp.arange(BUCKETS, dtype=jnp.int32)[None, None, :]).astype(jnp.int32)
    ranks = jnp.sum((jnp.cumsum(hits, axis=1) - 1) * hits, axis=2)
    counts = jnp.sum(hits, axis=1).reshape(BUCKETS, MEMBERS, BUCKETS)
    offsets = (jnp.cumsum(counts, axis=0) - counts).reshape(BUCKETS * MEMBERS, BUCKETS)
    arrival = jnp.take_along_axis(offsets, destination, axis=1) + ranks

    def one_receiver(receiver):
        return jax.random.permutation(jax.random.fold_in(jax.random.fold_in(base_key, 3), receiver), ROWS_DEV).astype(jnp.int32)
    slot_perm = jax.vmap(one_receiver)(senders)
    member_of = (senders % MEMBERS)[:, None]
    flat_index = ((destination * MEMBERS + member_of) * ROWS_DEV + arrival).reshape(-1)
    slots = slot_perm.reshape(-1)[flat_index]
    return (destination.reshape(-1).astype(jnp.int32), slots.astype(jnp.int32))


def draw_dest_bucket(key, part):
    return routing(key)[0]


def draw_dest_slot(key, part):
    return routing(key)[1]


def draw_loader_rows(key, part):
    base_key = jax.random.fold_in(key, 7)
    value_key = jax.random.fold_in(base_key, 1)
    scale_key = jax.random.fold_in(base_key, 2)
    values = jnp.clip(jax.random.normal(value_key, (LOAD_TOTAL, D), jnp.float32), -6.0, 6.0)
    scales = jnp.exp(jax.random.uniform(scale_key, (LOAD_TOTAL, 1), jnp.float32, math.log(0.5), math.log(2.0)))
    return values * scales


def levels(stream_key, shape, shards, smallest, top_value):
    factor_of = 1.0
    for position, blocks in shards:
        heights = jax.random.uniform(jax.random.fold_in(jax.random.fold_in(stream_key, 6), position), (blocks,), jnp.float32, smallest / len(shards), top_value / len(shards))
        factor_of = factor_of * jnp.repeat(jnp.exp(heights), shape[position] // blocks).reshape((-1,) + (1,) * (len(shape) - 1 - position))
    return factor_of


def centred(rng, extent, width, most, pieces=(), held_as=jnp.bfloat16):
    loudness = levels(rng, extent, pieces, -0.22, 0.18) if pieces else 1.0
    drawn = jax.random.normal(rng, extent, jnp.float32) * width * loudness
    return jnp.minimum(jnp.maximum(drawn, -most), most).astype(held_as)


def setup_inputs(seed: int = 0) -> dict:
    key_list = jax.random.split(jax.random.key(seed), 5)
    loader_rows = draw_loader_rows(jax.random.fold_in(key_list[4], 71), 0)
    dest_bucket = draw_dest_bucket(jax.random.fold_in(key_list[4], 71), 0)
    dest_slot = draw_dest_slot(jax.random.fold_in(key_list[4], 71), 0)
    noise = centred(key_list[3], (BUCKETS * NOISE_TOTAL, D), 2.0, 12.0, ((0, 128),), jnp.float32)
    return {"loader_rows": loader_rows, "dest_bucket": dest_bucket, "dest_slot": dest_slot, "noise": noise}


def coupling(bundle):
    data_rows, live_rows, noise_rows = bundle
    epsilon = 0.64 / math.sqrt(D)
    cross_term = jnp.dot(data_rows, noise_rows.T, preferred_element_type=jnp.float32)
    data_wide = data_rows.astype(jnp.float32)
    noise_wide = noise_rows.astype(jnp.float32)
    cost_tile = (lax.optimization_barrier(jnp.sum(data_wide * data_wide, axis=1))[:, None] + lax.optimization_barrier(jnp.sum(noise_wide * noise_wide, axis=1))[None, :] - 2.0 * cross_term) / D
    alive_rows = live_rows > 0.5
    col_pot = jnp.zeros((cost_tile.shape[1],), jnp.float32)
    exponent = jnp.zeros(cost_tile.shape, jnp.float32)
    col_total = jnp.ones((cost_tile.shape[1],), jnp.float32)
    for sweep_index in range(ITERS):
        scores = (col_pot[None, :] - cost_tile) / epsilon
        row_peak = lax.optimization_barrier(jnp.max(scores, axis=1))
        row_total = lax.optimization_barrier(jnp.sum(jnp.exp(scores - row_peak[:, None]), axis=1))
        row_pot = -epsilon * (row_peak + jnp.log(row_total))
        col_scores = (row_pot[:, None] - cost_tile) / epsilon
        col_peak = lax.optimization_barrier(jnp.max(jnp.where(alive_rows[:, None], col_scores, -jnp.inf), axis=0))
        exponent = jnp.where(alive_rows[:, None], jnp.exp(col_scores - col_peak[None, :]), 0.0)
        col_total = lax.optimization_barrier(jnp.sum(exponent, axis=0))
        col_pot = -epsilon * (col_peak + jnp.log(col_total))
    weights = (exponent / col_total[None, :]).astype(jnp.bfloat16)
    return jnp.dot(weights.T, data_rows, preferred_element_type=jnp.float32)

def reference(loader_rows, dest_bucket, dest_slot, noise):
    rounded = loader_rows.astype(jnp.bfloat16)
    row_index = jnp.arange(LOAD_TOTAL, dtype=jnp.int32)
    member_index = row_index // LOAD_DEV % MEMBERS
    placed = (dest_bucket * ROWS_TOTAL + member_index * ROWS_DEV + dest_slot).astype(jnp.int32)
    data_rows = jnp.zeros((BUCKETS * ROWS_TOTAL, D), jnp.bfloat16).at[placed].set(rounded)
    live_rows = jnp.zeros((BUCKETS * ROWS_TOTAL,), jnp.bfloat16).at[placed].set(jnp.ones((LOAD_TOTAL,), jnp.bfloat16))
    noise_rows = noise.astype(jnp.bfloat16)
    targets = lax.map(coupling, (data_rows.reshape(BUCKETS, ROWS_TOTAL, D), live_rows.reshape(BUCKETS, ROWS_TOTAL), noise_rows.reshape(BUCKETS, NOISE_TOTAL, D)))
    return targets.reshape(BUCKETS * NOISE_TOTAL, D)
```

```python
import functools
import math

import jax
import jax.numpy as jnp
from jax import lax
from jax.experimental import pallas as pl
from jax.experimental.pallas import tpu as pltpu
from jax.sharding import PartitionSpec as P

ROWS_DEV = 128
ITERS = 4
SIDE = 4
LANES = 128
EMPTY = 16384.0
MESH = pl.DeviceIdType.MESH
CONTRACT_LAST = (((1,), (1,)), ((), ()))


def pairing_kernel(
    width,
    xs_ref,
    live_ref,
    noise_ref,
    out_ref,
    rows,
    cost,
    noise_wide,
    noise_rows,
    row_norm,
    col_shift,
    row_shift,
    weights,
    lse_out,
    lse_in,
    noise_sem,
    own_sem,
    first_send,
    first_recv,
    second_send,
    second_recv,
    lse_send,
    lse_recv,
):
    members = SIDE * SIDE
    capacity = xs_ref.shape[1]
    noise_count = noise_wide.shape[0]
    part_width = width // members
    tiles = capacity // LANES
    scale = 1.0 / (width * (0.64 / math.sqrt(width)))
    me = lax.axis_index("member")
    my_z, my_x = me // SIDE, me % SIDE

    def member_at(part, first, second):
        along_x, along_z = (first, second) if part == 0 else (second, first)
        return ((my_z + along_z + SIDE) % SIDE) * SIDE + (my_x + along_x + SIDE) % SIDE

    chunk = width // 4
    noise_copies = []
    for k in range(4):
        copy = pltpu.make_async_copy(
            noise_ref.at[:, pl.ds(k * chunk, chunk)],
            noise_wide.at[:, pl.ds(k * chunk, chunk)],
            noise_sem.at[k],
        )
        copy.start()
        noise_copies.append(copy)
    own_copy = pltpu.make_async_copy(xs_ref, rows.at[me], own_sem)
    own_copy.start()

    barrier = pltpu.get_barrier_semaphore()
    for k in range(1, members):
        pl.semaphore_signal(
            barrier, inc=1, device_id={"member": (me + k) % members}, device_id_type=MESH
        )
    pl.semaphore_wait(barrier, members - 1)

    half, quarter = capacity // 2, capacity // 4
    units = [(0, 0, capacity), (-1, 0, capacity), (1, 0, capacity), (2, 0, half), (2, half, half)]
    ways = (1, -1)
    pending = {}

    def send(label, part, owner, start, count, neighbour, sems, own=False):
        source = xs_ref.at[part] if own else rows.at[owner, part]
        copy = pltpu.make_async_remote_copy(
            src_ref=source.at[pl.ds(start, count)],
            dst_ref=rows.at[owner, part, pl.ds(start, count)],
            send_sem=sems[0],
            recv_sem=sems[1],
            device_id={"member": neighbour},
            device_id_type=MESH,
        )
        copy.start()
        pending[label] = copy

    def first_hop(part, d):
        sems = (first_send.at[part, 0, d], first_recv.at[part, 0, d])
        send(("f1", part, d), part, me, 0, capacity, member_at(part, ways[d], 0), sems, True)

    def first_forward(part, d):
        sems = (first_send.at[part, 1, d], first_recv.at[part, 1, d])
        owner = member_at(part, -ways[d], 0)
        send(("f2", part, d), part, owner, d * half, half, member_at(part, ways[d], 0), sems)

    def second_hop(part, u, d):
        first, start, count = units[u]
        sems = (second_send.at[part, 0, u, d], second_recv.at[part, 0, u, d])
        owner = me if u == 0 else member_at(part, first, 0)
        send(("g1", part, u, d), part, owner, start, count, member_at(part, 0, ways[d]), sems, u == 0)

    def second_forward(part, u, d):
        first, start, count = units[u]
        sems = (second_send.at[part, 1, u, d], second_recv.at[part, 1, u, d])
        owner = member_at(part, first, -ways[d])
        send(
            ("g2", part, u, d), part, owner, start + d * (count // 2), count // 2,
            member_at(part, 0, ways[d]), sems,
        )

    def arrive(label):
        pending[label].wait_recv()

    def add_slice(owner):
        panel = jnp.concatenate([rows[owner, 0], rows[owner, 1]], axis=1)
        cost[...] += lax.dot_general(
            noise_rows[owner], panel, CONTRACT_LAST, preferred_element_type=jnp.float32
        )
        wide = panel.astype(jnp.float32)
        square = wide * wide
        high = square.astype(jnp.bfloat16)
        low = (square - high.astype(jnp.float32)).astype(jnp.bfloat16)
        ones = jnp.ones((8, panel.shape[1]), jnp.bfloat16)
        row_norm[...] += lax.dot_general(
            ones, high, CONTRACT_LAST, preferred_element_type=jnp.float32
        ) + lax.dot_general(ones, low, CONTRACT_LAST, preferred_element_type=jnp.float32)

    for part in range(2):
        for d in range(2):
            first_hop(part, d)
    for part in range(2):
        for d in range(2):
            second_hop(part, 0, d)

    cost[...] = jnp.zeros_like(cost)
    row_norm[...] = jnp.zeros_like(row_norm)
    per_chunk = chunk // part_width
    noise_norm = jnp.zeros((noise_count, 1), jnp.float32)
    for k in range(4):
        noise_copies[k].wait()
        for s in range(per_chunk):
            q = k * per_chunk + s
            block = noise_wide[:, q * part_width : (q + 1) * part_width].astype(jnp.bfloat16)
            noise_rows[q] = block
            wide = block.astype(jnp.float32)
            noise_norm += jnp.sum(wide * wide, axis=1, keepdims=True)
    own_copy.wait()
    add_slice(me)

    for part in range(2):
        for d in range(2):
            arrive(("f1", part, d))
            first_forward(part, d)
            u = 1 if d == 0 else 2
            for e in range(2):
                second_hop(part, u, e)
    for part in range(2):
        for d in range(2):
            arrive(("g1", part, 0, d))
            second_forward(part, 0, d)
    for step in ways:
        add_slice(member_at(0, step, 0))
        add_slice(member_at(0, 0, step))
    for d in range(2):
        for part in range(2):
            arrive(("f2", part, d))
            for e in range(2):
                second_hop(part, 3 + d, e)
    for u in (1, 2):
        for part in range(2):
            for d in range(2):
                arrive(("g1", part, u, d))
                second_forward(part, u, d)
    for step in ways:
        for other in ways:
            add_slice(member_at(0, step, other))
    for u in (3, 4):
        for part in range(2):
            for d in range(2):
                arrive(("g1", part, u, d))
                second_forward(part, u, d)
    for part in range(2):
        for d in range(2):
            arrive(("g2", part, 0, d))
    for part in range(2):
        add_slice(member_at(part, 2, 0))
    for u in (1, 2):
        for part in range(2):
            for d in range(2):
                arrive(("g2", part, u, d))
        for part in range(2):
            add_slice(member_at(part, units[u][0], 2))
    for u in (3, 4):
        for part in range(2):
            for d in range(2):
                arrive(("g2", part, u, d))
    add_slice(member_at(0, 2, 2))
    for copy in pending.values():
        copy.wait_send()

    for t in range(tiles):
        lanes = slice(t * LANES, (t + 1) * LANES)
        cost[:, lanes] = (2.0 * cost[:, lanes] - row_norm[0:1, lanes] - noise_norm) * scale

    col_shift[...] = jnp.zeros_like(col_shift)
    row_chunk = 32
    for it in range(ITERS):
        for t in range(tiles):
            lanes = slice(t * LANES, (t + 1) * LANES)
            scores = cost[:, lanes] + col_shift[...]
            peak = jnp.max(scores, axis=0, keepdims=True)
            total = jnp.sum(jnp.exp(scores - peak), axis=0, keepdims=True)
            lse_out[it, t : t + 1, :] = peak + jnp.log(total)
        lse_copies = []
        for k in range(1, members):
            copy = pltpu.make_async_remote_copy(
                src_ref=lse_out.at[it],
                dst_ref=lse_in.at[it, k],
                send_sem=lse_send.at[it, k],
                recv_sem=lse_recv.at[it, k],
                device_id={"member": (me + k) % members},
                device_id_type=MESH,
            )
            copy.start()
            lse_copies.append(copy)
        for copy in lse_copies:
            copy.wait_recv()
        peak = lse_out[it]
        for k in range(1, members):
            peak = jnp.maximum(peak, lse_in[it, k])
        total = jnp.exp(lse_out[it] - peak)
        for k in range(1, members):
            total += jnp.exp(lse_in[it, k] - peak)
        shift = -(peak + jnp.log(total))
        for t in range(tiles):
            lanes = slice(t * LANES, (t + 1) * LANES)
            row_shift[0:1, lanes] = jnp.where(live_ref[0:1, lanes] > 0.5, shift[t : t + 1, :], -jnp.inf)
        for c in range(noise_count // row_chunk):
            span = slice(c * row_chunk, (c + 1) * row_chunk)
            scores = cost[span, :] + row_shift[0:1, :]
            peak = jnp.max(scores, axis=1, keepdims=True)
            exponent = jnp.exp(scores - peak)
            total = jnp.sum(exponent, axis=1, keepdims=True)
            if it < ITERS - 1:
                col_shift[span, :] = jnp.broadcast_to(-(peak + jnp.log(total)), (row_chunk, LANES))
            else:
                weights[span, :] = (exponent / total).astype(jnp.bfloat16)
        for copy in lse_copies:
            copy.wait_send()

    @pl.loop(0, members)
    def _(q):
        panel = jnp.concatenate([rows[q, 0], rows[q, 1]], axis=1)
        start = pl.multiple_of(q * part_width, part_width)
        out_ref[:, pl.ds(start, part_width)] = jnp.dot(
            weights[...], panel, preferred_element_type=jnp.float32
        )


def pair(xs, live, noise):
    members = SIDE * SIDE
    capacity = xs.shape[1]
    noise_count, width = noise.shape
    tiles = capacity // LANES
    part_width = width // members
    dma = pltpu.SemaphoreType.DMA
    return pl.pallas_call(
        functools.partial(pairing_kernel, width),
        out_shape=jax.ShapeDtypeStruct((noise_count, width), jnp.float32),
        in_specs=[
            pl.BlockSpec(memory_space=pltpu.VMEM),
            pl.BlockSpec(memory_space=pltpu.VMEM),
            pl.BlockSpec(memory_space=pl.ANY),
        ],
        out_specs=pl.BlockSpec(memory_space=pltpu.VMEM),
        scratch_shapes=[
            pltpu.VMEM((members, 2, capacity, LANES), jnp.bfloat16),
            pltpu.VMEM((noise_count, capacity), jnp.float32),
            pltpu.VMEM((noise_count, width), jnp.float32),
            pltpu.VMEM((members, noise_count, part_width), jnp.bfloat16),
            pltpu.VMEM((8, capacity), jnp.float32),
            pltpu.VMEM((noise_count, LANES), jnp.float32),
            pltpu.VMEM((8, capacity), jnp.float32),
            pltpu.VMEM((noise_count, capacity), jnp.bfloat16),
            pltpu.VMEM((ITERS, tiles, LANES), jnp.float32),
            pltpu.VMEM((ITERS, members, tiles, LANES), jnp.float32),
            dma((4,)),
            dma,
            dma((2, 2, 2)),
            dma((2, 2, 2)),
            dma((2, 2, 5, 2)),
            dma((2, 2, 5, 2)),
            dma((ITERS, members)),
            dma((ITERS, members)),
        ],
        compiler_params=pltpu.CompilerParams(
            collective_id=0, has_side_effects=True, vmem_limit_bytes=60 * 1024 * 1024
        ),
    )(xs, live, noise)


def body(loader_rows, dest_bucket, dest_slot, noise):
    groups = lax.axis_size("bucket")
    members = lax.axis_size("member")
    loaded, width = loader_rows.shape
    capacity = ROWS_DEV // groups
    rounded = loader_rows.astype(jnp.bfloat16)
    index = jnp.arange(loaded, dtype=jnp.int32)
    earlier = (dest_bucket[:, None] == dest_bucket[None, :]) & (index[None, :] < index[:, None])
    position = dest_bucket * capacity + jnp.sum(earlier.astype(jnp.int32), axis=1)
    hits = position[None, :] == jnp.arange(groups * capacity, dtype=jnp.int32)[:, None]
    packed = jnp.dot(hits.astype(jnp.bfloat16), rounded, preferred_element_type=jnp.float32)
    filled = jnp.any(hits, axis=1)
    packed = jnp.where(filled[:, None], packed, EMPTY).astype(jnp.bfloat16)
    packed = packed.reshape(groups, capacity, members, width // members)
    packed = packed.transpose(0, 2, 1, 3).reshape(groups * members, capacity, width // members)
    got = lax.all_to_all(packed, ("bucket", "member"), split_axis=0, concat_axis=0, tiled=True)
    got = got.reshape(groups * members * capacity, width // members)
    live = got[:, 0] < 0.5 * EMPTY
    got = jnp.where(live[:, None], got, jnp.zeros_like(got))
    xs = jnp.stack([got[:, :LANES], got[:, LANES:]])
    live_rows = jnp.broadcast_to(live.astype(jnp.float32)[None, :], (8, live.shape[0]))
    return pair(xs, live_rows, noise)


def solution(mesh):
    return jax.shard_map(
        body,
        mesh=mesh,
        in_specs=(
            P(("bucket", "member"), None),
            P(("bucket", "member")),
            P(("bucket", "member")),
            P(("bucket", "member"), None),
        ),
        out_specs=P(("bucket", "member"), None),
        check_vma=False,
    )
```

```python
import functools
import math

import jax
import jax.numpy as jnp
from jax import lax
from jax.experimental import pallas as pl
from jax.experimental.pallas import tpu as pltpu
from jax.sharding import PartitionSpec as P

ROWS_DEV = 128
ITERS = 4
SIDE = 4
BUCKETS = 8
FAST_ROWS = 1152
LANES = 128
EMPTY = 16384.0
MESH = pl.DeviceIdType.MESH
CONTRACT_LAST = (((1,), (1,)), ((), ()))


def pairing_kernel(
    width,
    xs_ref,
    live_ref,
    noise_ref,
    out_ref,
    rows,
    cost,
    noise_wide,
    noise_rows,
    row_norm,
    col_shift,
    row_shift,
    weights,
    lse_out,
    lse_in,
    noise_sem,
    own_sem,
    first_send,
    first_recv,
    second_send,
    second_recv,
    lse_send,
    lse_recv,
):
    members = SIDE * SIDE
    capacity = xs_ref.shape[1]
    noise_count = noise_wide.shape[0]
    part_width = width // members
    tiles = capacity // LANES
    scale = 1.0 / (width * (0.64 / math.sqrt(width)))
    me = lax.axis_index("member")
    my_z, my_x = me // SIDE, me % SIDE

    def member_at(part, first, second):
        along_x, along_z = (first, second) if part == 0 else (second, first)
        return ((my_z + along_z + SIDE) % SIDE) * SIDE + (my_x + along_x + SIDE) % SIDE

    chunk = width // 4
    noise_copies = []
    for k in range(4):
        copy = pltpu.make_async_copy(
            noise_ref.at[:, pl.ds(k * chunk, chunk)],
            noise_wide.at[:, pl.ds(k * chunk, chunk)],
            noise_sem.at[k],
        )
        copy.start()
        noise_copies.append(copy)
    own_copy = pltpu.make_async_copy(xs_ref, rows.at[me], own_sem)
    own_copy.start()

    barrier = pltpu.get_barrier_semaphore()
    for k in range(1, members):
        pl.semaphore_signal(
            barrier, inc=1, device_id={"member": (me + k) % members}, device_id_type=MESH
        )
    pl.semaphore_wait(barrier, members - 1)

    half, quarter = capacity // 2, capacity // 4
    units = [(0, 0, capacity), (-1, 0, capacity), (1, 0, capacity), (2, 0, half), (2, half, half)]
    ways = (1, -1)
    pending = {}

    def send(label, part, owner, start, count, neighbour, sems, own=False):
        source = xs_ref.at[part] if own else rows.at[owner, part]
        copy = pltpu.make_async_remote_copy(
            src_ref=source.at[pl.ds(start, count)],
            dst_ref=rows.at[owner, part, pl.ds(start, count)],
            send_sem=sems[0],
            recv_sem=sems[1],
            device_id={"member": neighbour},
            device_id_type=MESH,
        )
        copy.start()
        pending[label] = copy

    def first_hop(part, d):
        sems = (first_send.at[part, 0, d], first_recv.at[part, 0, d])
        send(("f1", part, d), part, me, 0, capacity, member_at(part, ways[d], 0), sems, True)

    def first_forward(part, d):
        sems = (first_send.at[part, 1, d], first_recv.at[part, 1, d])
        owner = member_at(part, -ways[d], 0)
        send(("f2", part, d), part, owner, d * half, half, member_at(part, ways[d], 0), sems)

    def second_hop(part, u, d):
        first, start, count = units[u]
        sems = (second_send.at[part, 0, u, d], second_recv.at[part, 0, u, d])
        owner = me if u == 0 else member_at(part, first, 0)
        send(("g1", part, u, d), part, owner, start, count, member_at(part, 0, ways[d]), sems, u == 0)

    def second_forward(part, u, d):
        first, start, count = units[u]
        sems = (second_send.at[part, 1, u, d], second_recv.at[part, 1, u, d])
        owner = member_at(part, first, -ways[d])
        send(
            ("g2", part, u, d), part, owner, start + d * (count // 2), count // 2,
            member_at(part, 0, ways[d]), sems,
        )

    def arrive(label):
        pending[label].wait_recv()

    def add_slice(owner):
        panel = jnp.concatenate([rows[owner, 0], rows[owner, 1]], axis=1)
        cost[...] += lax.dot_general(
            noise_rows[owner], panel, CONTRACT_LAST, preferred_element_type=jnp.float32
        )
        wide = panel.astype(jnp.float32)
        square = wide * wide
        high = square.astype(jnp.bfloat16)
        low = (square - high.astype(jnp.float32)).astype(jnp.bfloat16)
        ones = jnp.ones((8, panel.shape[1]), jnp.bfloat16)
        row_norm[...] += lax.dot_general(
            ones, high, CONTRACT_LAST, preferred_element_type=jnp.float32
        ) + lax.dot_general(ones, low, CONTRACT_LAST, preferred_element_type=jnp.float32)

    for part in range(2):
        for d in range(2):
            first_hop(part, d)
    for part in range(2):
        for d in range(2):
            second_hop(part, 0, d)

    cost[...] = jnp.zeros_like(cost)
    row_norm[...] = jnp.zeros_like(row_norm)
    per_chunk = chunk // part_width
    noise_norm = jnp.zeros((noise_count, 1), jnp.float32)
    for k in range(4):
        noise_copies[k].wait()
        for s in range(per_chunk):
            q = k * per_chunk + s
            block = noise_wide[:, q * part_width : (q + 1) * part_width].astype(jnp.bfloat16)
            noise_rows[q] = block
            wide = block.astype(jnp.float32)
            noise_norm += jnp.sum(wide * wide, axis=1, keepdims=True)
    own_copy.wait()
    add_slice(me)

    for part in range(2):
        for d in range(2):
            arrive(("f1", part, d))
            first_forward(part, d)
            u = 1 if d == 0 else 2
            for e in range(2):
                second_hop(part, u, e)
    for part in range(2):
        for d in range(2):
            arrive(("g1", part, 0, d))
            second_forward(part, 0, d)
    for step in ways:
        add_slice(member_at(0, step, 0))
        add_slice(member_at(0, 0, step))
    for d in range(2):
        for part in range(2):
            arrive(("f2", part, d))
            for e in range(2):
                second_hop(part, 3 + d, e)
    for u in (1, 2):
        for part in range(2):
            for d in range(2):
                arrive(("g1", part, u, d))
                second_forward(part, u, d)
    for step in ways:
        for other in ways:
            add_slice(member_at(0, step, other))
    for u in (3, 4):
        for part in range(2):
            for d in range(2):
                arrive(("g1", part, u, d))
                second_forward(part, u, d)
    for part in range(2):
        for d in range(2):
            arrive(("g2", part, 0, d))
    for part in range(2):
        add_slice(member_at(part, 2, 0))
    for u in (1, 2):
        for part in range(2):
            for d in range(2):
                arrive(("g2", part, u, d))
        for part in range(2):
            add_slice(member_at(part, units[u][0], 2))
    for u in (3, 4):
        for part in range(2):
            for d in range(2):
                arrive(("g2", part, u, d))
    add_slice(member_at(0, 2, 2))
    for copy in pending.values():
        copy.wait_send()

    for t in range(tiles):
        lanes = slice(t * LANES, (t + 1) * LANES)
        cost[:, lanes] = (2.0 * cost[:, lanes] - row_norm[0:1, lanes] - noise_norm) * scale

    col_shift[...] = jnp.zeros_like(col_shift)
    row_chunk = 32
    for it in range(ITERS):
        for t in range(tiles):
            lanes = slice(t * LANES, (t + 1) * LANES)
            scores = cost[:, lanes] + col_shift[...]
            peak = jnp.max(scores, axis=0, keepdims=True)
            total = jnp.sum(jnp.exp(scores - peak), axis=0, keepdims=True)
            lse_out[it, t : t + 1, :] = peak + jnp.log(total)
        lse_copies = []
        for k in range(1, members):
            copy = pltpu.make_async_remote_copy(
                src_ref=lse_out.at[it],
                dst_ref=lse_in.at[it, k],
                send_sem=lse_send.at[it, k],
                recv_sem=lse_recv.at[it, k],
                device_id={"member": (me + k) % members},
                device_id_type=MESH,
            )
            copy.start()
            lse_copies.append(copy)
        for copy in lse_copies:
            copy.wait_recv()
        peak = lse_out[it]
        for k in range(1, members):
            peak = jnp.maximum(peak, lse_in[it, k])
        total = jnp.exp(lse_out[it] - peak)
        for k in range(1, members):
            total += jnp.exp(lse_in[it, k] - peak)
        shift = -(peak + jnp.log(total))
        for t in range(tiles):
            lanes = slice(t * LANES, (t + 1) * LANES)
            row_shift[0:1, lanes] = jnp.where(live_ref[0:1, lanes] > 0.5, shift[t : t + 1, :], -jnp.inf)
        for c in range(noise_count // row_chunk):
            span = slice(c * row_chunk, (c + 1) * row_chunk)
            scores = cost[span, :] + row_shift[0:1, :]
            peak = jnp.max(scores, axis=1, keepdims=True)
            exponent = jnp.exp(scores - peak)
            total = jnp.sum(exponent, axis=1, keepdims=True)
            if it < ITERS - 1:
                col_shift[span, :] = jnp.broadcast_to(-(peak + jnp.log(total)), (row_chunk, LANES))
            else:
                weights[span, :] = (exponent / total).astype(jnp.bfloat16)
        for copy in lse_copies:
            copy.wait_send()

    @pl.loop(0, members)
    def _(q):
        panel = jnp.concatenate([rows[q, 0], rows[q, 1]], axis=1)
        start = pl.multiple_of(q * part_width, part_width)
        out_ref[:, pl.ds(start, part_width)] = jnp.dot(
            weights[...], panel, preferred_element_type=jnp.float32
        )


def pair(xs, live, noise, collective_id):
    members = SIDE * SIDE
    capacity = xs.shape[1]
    noise_count, width = noise.shape
    tiles = capacity // LANES
    part_width = width // members
    dma = pltpu.SemaphoreType.DMA
    return pl.pallas_call(
        functools.partial(pairing_kernel, width),
        out_shape=jax.ShapeDtypeStruct((noise_count, width), jnp.float32),
        in_specs=[
            pl.BlockSpec(memory_space=pltpu.VMEM),
            pl.BlockSpec(memory_space=pltpu.VMEM),
            pl.BlockSpec(memory_space=pl.ANY),
        ],
        out_specs=pl.BlockSpec(memory_space=pltpu.VMEM),
        scratch_shapes=[
            pltpu.VMEM((members, 2, capacity, LANES), jnp.bfloat16),
            pltpu.VMEM((noise_count, capacity), jnp.float32),
            pltpu.VMEM((noise_count, width), jnp.float32),
            pltpu.VMEM((members, noise_count, part_width), jnp.bfloat16),
            pltpu.VMEM((8, capacity), jnp.float32),
            pltpu.VMEM((noise_count, LANES), jnp.float32),
            pltpu.VMEM((8, capacity), jnp.float32),
            pltpu.VMEM((noise_count, capacity), jnp.bfloat16),
            pltpu.VMEM((ITERS, tiles, LANES), jnp.float32),
            pltpu.VMEM((ITERS, members, tiles, LANES), jnp.float32),
            dma((4,)),
            dma,
            dma((2, 2, 2)),
            dma((2, 2, 2)),
            dma((2, 2, 5, 2)),
            dma((2, 2, 5, 2)),
            dma((ITERS, members)),
            dma((ITERS, members)),
        ],
        compiler_params=pltpu.CompilerParams(
            collective_id=collective_id, has_side_effects=True, vmem_limit_bytes=60 * 1024 * 1024
        ),
    )(xs, live, noise)


def routing_kernel(
    dest_ref,
    loaded_ref,
    slots_ref,
    live_ref,
    count_ref,
    packed,
    landed,
    position,
    tally,
    tally_bucket,
    tally_member,
    bucket_send,
    bucket_recv,
    member_send,
    member_recv,
    tally_send,
    tally_recv,
):
    groups, members = BUCKETS, SIDE * SIDE
    loaded, width = loaded_ref.shape
    part_width = width // members
    block = ROWS_DEV // groups
    fast_rows = live_ref.shape[1]
    my_bucket, me = lax.axis_index("bucket"), lax.axis_index("member")

    barrier = pltpu.get_barrier_semaphore()
    for k in range(1, groups):
        pl.semaphore_signal(
            barrier, inc=1, device_id={"bucket": (my_bucket + k) % groups}, device_id_type=MESH
        )
    for k in range(1, members):
        pl.semaphore_signal(
            barrier, inc=1, device_id={"member": (me + k) % members}, device_id_type=MESH
        )

    dest = dest_ref[...]
    of_bucket = lax.broadcasted_iota(jnp.int32, (groups, loaded), 0) == dest
    hits = of_bucket.astype(jnp.float32)
    up_to = (
        lax.broadcasted_iota(jnp.int32, (loaded, loaded), 0)
        <= lax.broadcasted_iota(jnp.int32, (loaded, loaded), 1)
    ).astype(jnp.bfloat16)
    ranks = jnp.dot(hits.astype(jnp.bfloat16), up_to, preferred_element_type=jnp.float32)
    place = jnp.sum(hits * (ranks - 1.0), axis=0, keepdims=True).astype(jnp.int32) + dest * block
    pick = lax.broadcasted_iota(jnp.int32, (ROWS_DEV, loaded), 0) == place
    pick = pick.astype(jnp.float32)
    fill = EMPTY * (1.0 - jnp.sum(pick, axis=1, keepdims=True))
    pick = pick.astype(jnp.bfloat16)
    tally[0] = jnp.broadcast_to(jnp.sum(hits, axis=1, keepdims=True), tally.shape[1:])

    def pack(c):
        for k in range(4 * c, 4 * c + 4):
            start = pl.multiple_of(((me + k) % members) * part_width, part_width)
            panel = loaded_ref[:, pl.ds(start, part_width)].astype(jnp.bfloat16)
            sorted_panel = jnp.dot(pick, panel, preferred_element_type=jnp.float32) + fill
            sorted_panel = sorted_panel.astype(jnp.bfloat16)
            for part in range(2):
                packed[k, part] = sorted_panel[:, part * LANES : (part + 1) * LANES]

    def block_of(bucket):
        return pl.ds(pl.multiple_of(bucket * block, block), block)

    bucket_copies = {}

    def send_quarter(c):
        quarter = pl.ds(4 * c, 4)
        for k in range(1, groups):
            peer = (my_bucket + k) % groups
            copy = pltpu.make_async_remote_copy(
                src_ref=packed.at[quarter, :, block_of(peer)],
                dst_ref=landed.at[quarter, :, block_of(my_bucket)],
                send_sem=bucket_send.at[c, k],
                recv_sem=bucket_recv.at[c, k],
                device_id={"bucket": peer},
                device_id_type=MESH,
            )
            copy.start()
            bucket_copies[c, k] = copy
        landed[quarter, :, block_of(my_bucket), :] = packed[quarter, :, block_of(my_bucket), :]

    pack(0)
    pl.semaphore_wait(barrier, groups + members - 2)
    send_quarter(0)
    tally_copies = []
    for k in range(1, groups):
        copy = pltpu.make_async_remote_copy(
            src_ref=tally.at[0],
            dst_ref=tally_bucket.at[k],
            send_sem=tally_send.at[0, k],
            recv_sem=tally_recv.at[0, k],
            device_id={"bucket": (my_bucket + k) % groups},
            device_id_type=MESH,
        )
        copy.start()
        tally_copies.append(copy)
    for c in range(1, 4):
        pack(c)
        send_quarter(c)
    my_rows = pl.ds(pl.multiple_of(me * ROWS_DEV, ROWS_DEV), ROWS_DEV)
    member_copies = []
    for c in range(4):
        for k in range(1, groups):
            bucket_copies[c, k].wait_recv()
        for k in range(4 * c, 4 * c + 4):
            if k == 0:
                slots_ref[:, my_rows, :] = landed[0]
                continue
            copy = pltpu.make_async_remote_copy(
                src_ref=landed.at[k],
                dst_ref=slots_ref.at[:, my_rows],
                send_sem=member_send.at[k],
                recv_sem=member_recv.at[k],
                device_id={"member": (me + k) % members},
                device_id_type=MESH,
            )
            copy.start()
            member_copies.append(copy)
        if c == 0:
            total = tally[0]
            for k in range(1, groups):
                tally_copies[k - 1].wait_recv()
                total += tally_bucket[k]
            tally[1] = total
            for k in range(1, members):
                copy = pltpu.make_async_remote_copy(
                    src_ref=tally.at[1],
                    dst_ref=tally_member.at[k],
                    send_sem=tally_send.at[1, k],
                    recv_sem=tally_recv.at[1, k],
                    device_id={"member": (me + k) % members},
                    device_id_type=MESH,
                )
                copy.start()
                tally_copies.append(copy)
    total = tally[1]
    for k in range(1, members):
        tally_copies[groups - 2 + k].wait_recv()
        total += tally_member[k]
    count_ref[...] = total
    for copy in member_copies:
        copy.wait_recv()

    marks = lax.dot_general(
        jnp.ones((8, LANES), jnp.bfloat16), slots_ref[0], CONTRACT_LAST,
        preferred_element_type=jnp.float32,
    )
    for t in range(members):
        lanes = slice(t * LANES, (t + 1) * LANES)
        position[t : t + 1, :] = (marks[0:1, lanes] < 0.5 * LANES * EMPTY).astype(jnp.float32)
    alive = position[...]
    before = (
        lax.broadcasted_iota(jnp.int32, (LANES, LANES), 0)
        <= lax.broadcasted_iota(jnp.int32, (LANES, LANES), 1)
    ).astype(jnp.bfloat16)
    inside = jnp.dot(alive.astype(jnp.bfloat16), before, preferred_element_type=jnp.float32)
    per_member = jnp.broadcast_to(inside[:, LANES - 1 : LANES], (members, LANES))
    earlier = (
        lax.broadcasted_iota(jnp.int32, (members, members), 0)
        > lax.broadcasted_iota(jnp.int32, (members, members), 1)
    ).astype(jnp.bfloat16)
    offset = jnp.dot(earlier, per_member.astype(jnp.bfloat16), preferred_element_type=jnp.float32)
    position[...] = jnp.where(alive > 0.5, inside + offset - 1.0, -1.0)
    step = fast_rows // 3

    @pl.loop(0, 3)
    def _(c):
        start = pl.multiple_of(c * step, step)
        target = (lax.broadcasted_iota(jnp.int32, (step, LANES), 0) + start).astype(jnp.float32)
        choose = jnp.concatenate(
            [(target == position[t : t + 1, :]).astype(jnp.bfloat16) for t in range(members)], axis=1
        )
        for part in range(2):
            live_ref[part, pl.ds(start, step), :] = jnp.dot(
                choose, slots_ref[part], preferred_element_type=jnp.float32
            ).astype(jnp.bfloat16)

    for copy in list(bucket_copies.values()) + tally_copies + member_copies:
        copy.wait_send()


def route(dest_bucket, loader_rows):
    members = SIDE * SIDE
    width = loader_rows.shape[1]
    dma = pltpu.SemaphoreType.DMA
    vmem = pl.BlockSpec(memory_space=pltpu.VMEM)
    slot_rows = members * ROWS_DEV
    return pl.pallas_call(
        routing_kernel,
        out_shape=(
            jax.ShapeDtypeStruct((2, slot_rows, LANES), jnp.bfloat16),
            jax.ShapeDtypeStruct((2, FAST_ROWS, LANES), jnp.bfloat16),
            jax.ShapeDtypeStruct((BUCKETS, LANES), jnp.float32),
        ),
        in_specs=[vmem, vmem],
        out_specs=(vmem, vmem, vmem),
        scratch_shapes=[
            pltpu.VMEM((members, 2, ROWS_DEV, LANES), jnp.bfloat16),
            pltpu.VMEM((members, 2, ROWS_DEV, LANES), jnp.bfloat16),
            pltpu.VMEM((members, LANES), jnp.float32),
            pltpu.VMEM((2, BUCKETS, LANES), jnp.float32),
            pltpu.VMEM((BUCKETS, BUCKETS, LANES), jnp.float32),
            pltpu.VMEM((members, BUCKETS, LANES), jnp.float32),
            dma((4, BUCKETS)),
            dma((4, BUCKETS)),
            dma((members,)),
            dma((members,)),
            dma((2, members)),
            dma((2, members)),
        ],
        compiler_params=pltpu.CompilerParams(
            collective_id=1, has_side_effects=True, vmem_limit_bytes=40 * 1024 * 1024
        ),
    )(dest_bucket.reshape(1, -1), loader_rows)


def body(loader_rows, dest_bucket, dest_slot, noise):
    slots, compact, counts = route(dest_bucket, loader_rows)
    group = lax.axis_index("bucket")

    def all_slots(slots, compact, counts, noise):
        live = (slots[0, :, 0] < 0.5 * EMPTY).astype(jnp.float32)
        cleared = jnp.where(slots < 0.5 * EMPTY, slots, jnp.zeros_like(slots))
        return pair(cleared, jnp.broadcast_to(live[None, :], (8, live.shape[0])), noise, 2)

    def live_first(slots, compact, counts, noise):
        index = lax.broadcasted_iota(jnp.int32, (8, FAST_ROWS), 1).astype(jnp.float32)
        live = (index < counts[group, 0]).astype(jnp.float32)
        return pair(compact, live, noise, 0)

    fits = jnp.all(counts <= FAST_ROWS)
    return lax.cond(fits, live_first, all_slots, slots, compact, counts, noise)


def solution(mesh):
    return jax.shard_map(
        body,
        mesh=mesh,
        in_specs=(
            P(("bucket", "member"), None),
            P(("bucket", "member")),
            P(("bucket", "member")),
            P(("bucket", "member"), None),
        ),
        out_specs=P(("bucket", "member"), None),
        check_vma=False,
    )
```

```python
import functools
import math

import jax
import jax.numpy as jnp
from jax import lax
from jax.experimental import pallas as pl
from jax.experimental.pallas import tpu as pltpu
from jax.sharding import PartitionSpec as P

ROWS_DEV = 128
ITERS = 4
SIDE = 4
BUCKETS = 8
FAST_ROWS = 1120
LANES = 128
EMPTY = 16384.0
MESH = pl.DeviceIdType.MESH
CONTRACT_LAST = (((1,), (1,)), ((), ()))


def pairing_kernel(
    width,
    sent,
    slots_ref,
    count_ref,
    noise_ref,
    rows,
    weights,
    cost,
    noise_wide,
    noise_rows,
    row_norm,
    live,
    position,
    col_shift,
    row_shift,
    lse_out,
    lse_in,
    noise_sem,
    first_send,
    first_recv,
    second_send,
    second_recv,
    lse_send,
    lse_recv,
):
    members = SIDE * SIDE
    capacity = rows.shape[2]
    noise_count = noise_wide.shape[0]
    part_width = width // members
    tiles = capacity // LANES
    scale = 1.0 / (width * (0.64 / math.sqrt(width)))
    me = lax.axis_index("member")
    my_z, my_x = me // SIDE, me % SIDE

    def member_at(part, first, second):
        along_x, along_z = (first, second) if part == 0 else (second, first)
        return ((my_z + along_z + SIDE) % SIDE) * SIDE + (my_x + along_x + SIDE) % SIDE

    chunk = width // 4
    noise_copies = []
    for k in range(4):
        copy = pltpu.make_async_copy(
            noise_ref.at[:, pl.ds(k * chunk, chunk)],
            noise_wide.at[:, pl.ds(k * chunk, chunk)],
            noise_sem.at[k],
        )
        copy.start()
        noise_copies.append(copy)

    barrier = pltpu.get_barrier_semaphore()
    for k in range(1, members):
        pl.semaphore_signal(
            barrier, inc=1, device_id={"member": (me + k) % members}, device_id_type=MESH
        )

    marks = jnp.concatenate(
        [
            lax.dot_general(
                jnp.ones((8, LANES), jnp.bfloat16), slots_ref[0, t], CONTRACT_LAST,
                preferred_element_type=jnp.float32,
            )[0:1]
            for t in range(members)
        ],
        axis=0,
    )
    alive = (marks < 0.5 * LANES * EMPTY).astype(jnp.float32)
    if capacity == members * ROWS_DEV:
        live[...] = alive
        for part in range(2):
            for t in range(members):
                block = slots_ref[part, t].astype(jnp.float32)
                block = jnp.where(block < 0.5 * EMPTY, block, 0.0)
                rows[me, part, t * ROWS_DEV : (t + 1) * ROWS_DEV, :] = block.astype(jnp.bfloat16)
    else:
        before = (
            lax.broadcasted_iota(jnp.int32, (LANES, LANES), 0)
            <= lax.broadcasted_iota(jnp.int32, (LANES, LANES), 1)
        ).astype(jnp.bfloat16)
        inside = jnp.dot(alive.astype(jnp.bfloat16), before, preferred_element_type=jnp.float32)
        per_member = jnp.broadcast_to(inside[:, LANES - 1 : LANES], (members, LANES))
        earlier = (
            lax.broadcasted_iota(jnp.int32, (members, members), 0)
            > lax.broadcasted_iota(jnp.int32, (members, members), 1)
        ).astype(jnp.bfloat16)
        offset = jnp.dot(
            earlier, per_member.astype(jnp.bfloat16), preferred_element_type=jnp.float32
        )
        position[...] = jnp.where(alive > 0.5, inside + offset - 1.0, -1.0)
        step = capacity // 3

        @pl.loop(0, 3)
        def _(c):
            start = pl.multiple_of(c * step, LANES)
            target = (lax.broadcasted_iota(jnp.int32, (step, LANES), 0) + start).astype(jnp.float32)
            choose = jnp.concatenate(
                [(target == position[t : t + 1, :]).astype(jnp.bfloat16) for t in range(members)],
                axis=1,
            )
            both = jnp.concatenate(
                [slots_ref[part].reshape(members * ROWS_DEV, LANES) for part in range(2)], axis=1
            )
            chosen = jnp.dot(choose, both, preferred_element_type=jnp.float32).astype(jnp.bfloat16)
            for part in range(2):
                rows[me, part, pl.ds(start, step), :] = chosen[:, part * LANES : (part + 1) * LANES]

        held = count_ref[pl.ds(lax.axis_index("bucket"), 1), :]
        place = lax.broadcasted_iota(jnp.int32, (tiles, LANES), 0) * LANES
        place += lax.broadcasted_iota(jnp.int32, (tiles, LANES), 1)
        live[...] = (place.astype(jnp.float32) < held).astype(jnp.float32)
        if sent < capacity:
            blank = jnp.zeros((capacity - sent, LANES), jnp.bfloat16)
            for q in range(members):
                for part in range(2):
                    rows[q, part, sent:capacity, :] = blank
    pl.semaphore_wait(barrier, members - 1)

    def front(count):
        return -(-count // 32) * 16

    half = front(sent)
    units = [(0, 0, sent), (-1, 0, sent), (1, 0, sent), (2, 0, half), (2, half, sent - half)]
    ways = (1, -1)
    pending = {}

    def side(start, count, d):
        middle = front(count)
        return (start, middle) if d == 0 else (start + middle, count - middle)

    def send(label, part, owner, span, neighbour, sems):
        piece = rows.at[owner, part, pl.ds(*span)]
        copy = pltpu.make_async_remote_copy(
            src_ref=piece,
            dst_ref=piece,
            send_sem=sems[0],
            recv_sem=sems[1],
            device_id={"member": neighbour},
            device_id_type=MESH,
        )
        copy.start()
        pending[label] = copy

    def first_hop(part, d):
        sems = (first_send.at[part, 0, d], first_recv.at[part, 0, d])
        send(("f1", part, d), part, me, (0, sent), member_at(part, ways[d], 0), sems)

    def first_forward(part, d):
        sems = (first_send.at[part, 1, d], first_recv.at[part, 1, d])
        owner = member_at(part, -ways[d], 0)
        send(("f2", part, d), part, owner, side(0, sent, d), member_at(part, ways[d], 0), sems)

    def second_hop(part, u, d):
        first, start, count = units[u]
        sems = (second_send.at[part, 0, u, d], second_recv.at[part, 0, u, d])
        owner = me if u == 0 else member_at(part, first, 0)
        send(("g1", part, u, d), part, owner, (start, count), member_at(part, 0, ways[d]), sems)

    def second_forward(part, u, d):
        first, start, count = units[u]
        sems = (second_send.at[part, 1, u, d], second_recv.at[part, 1, u, d])
        owner = member_at(part, first, -ways[d])
        send(
            ("g2", part, u, d), part, owner, side(start, count, d), member_at(part, 0, ways[d]), sems
        )

    def arrive(label):
        pending[label].wait_recv()

    def add_slice(owner):
        panel = jnp.concatenate([rows[owner, 0], rows[owner, 1]], axis=1)
        cost[...] += lax.dot_general(
            noise_rows[owner], panel, CONTRACT_LAST, preferred_element_type=jnp.float32
        )
        wide = panel.astype(jnp.float32)
        square = wide * wide
        high = square.astype(jnp.bfloat16)
        low = (square - high.astype(jnp.float32)).astype(jnp.bfloat16)
        ones = jnp.ones((8, panel.shape[1]), jnp.bfloat16)
        row_norm[...] += lax.dot_general(
            ones, high, CONTRACT_LAST, preferred_element_type=jnp.float32
        ) + lax.dot_general(ones, low, CONTRACT_LAST, preferred_element_type=jnp.float32)

    for part in range(2):
        for d in range(2):
            first_hop(part, d)
    for part in range(2):
        for d in range(2):
            second_hop(part, 0, d)

    cost[...] = jnp.zeros_like(cost)
    row_norm[...] = jnp.zeros_like(row_norm)
    per_chunk = chunk // part_width
    noise_norm = jnp.zeros((noise_count, 1), jnp.float32)
    for k in range(4):
        noise_copies[k].wait()
        for s in range(per_chunk):
            q = k * per_chunk + s
            block = noise_wide[:, q * part_width : (q + 1) * part_width].astype(jnp.bfloat16)
            noise_rows[q] = block
            wide = block.astype(jnp.float32)
            noise_norm += jnp.sum(wide * wide, axis=1, keepdims=True)
    add_slice(me)

    for part in range(2):
        for d in range(2):
            arrive(("f1", part, d))
            first_forward(part, d)
            u = 1 if d == 0 else 2
            for e in range(2):
                second_hop(part, u, e)
    for part in range(2):
        for d in range(2):
            arrive(("g1", part, 0, d))
            second_forward(part, 0, d)
    for step in ways:
        add_slice(member_at(0, step, 0))
        add_slice(member_at(0, 0, step))
    for d in range(2):
        for part in range(2):
            arrive(("f2", part, d))
            for e in range(2):
                second_hop(part, 3 + d, e)
    for u in (1, 2):
        for part in range(2):
            for d in range(2):
                arrive(("g1", part, u, d))
                second_forward(part, u, d)
    for step in ways:
        for other in ways:
            add_slice(member_at(0, step, other))
    for u in (3, 4):
        for part in range(2):
            for d in range(2):
                arrive(("g1", part, u, d))
                second_forward(part, u, d)
    for part in range(2):
        for d in range(2):
            arrive(("g2", part, 0, d))
    for part in range(2):
        add_slice(member_at(part, 2, 0))
    for u in (1, 2):
        for part in range(2):
            for d in range(2):
                arrive(("g2", part, u, d))
        for part in range(2):
            add_slice(member_at(part, units[u][0], 2))
    for u in (3, 4):
        for part in range(2):
            for d in range(2):
                arrive(("g2", part, u, d))
    add_slice(member_at(0, 2, 2))
    for copy in pending.values():
        copy.wait_send()

    for t in range(tiles):
        lanes = slice(t * LANES, (t + 1) * LANES)
        cost[:, lanes] = (2.0 * cost[:, lanes] - row_norm[0:1, lanes] - noise_norm) * scale

    col_shift[...] = jnp.zeros_like(col_shift)
    row_chunk = 32
    for it in range(ITERS):
        for t in range(tiles):
            lanes = slice(t * LANES, (t + 1) * LANES)
            scores = cost[:, lanes] + col_shift[...]
            peak = jnp.max(scores, axis=0, keepdims=True)
            total = jnp.sum(jnp.exp(scores - peak), axis=0, keepdims=True)
            lse_out[it, t : t + 1, :] = peak + jnp.log(total)
        lse_copies = []
        for k in range(1, members):
            copy = pltpu.make_async_remote_copy(
                src_ref=lse_out.at[it],
                dst_ref=lse_in.at[it, k],
                send_sem=lse_send.at[it, k],
                recv_sem=lse_recv.at[it, k],
                device_id={"member": (me + k) % members},
                device_id_type=MESH,
            )
            copy.start()
            lse_copies.append(copy)
        for copy in lse_copies:
            copy.wait_recv()
        peak = lse_out[it]
        for k in range(1, members):
            peak = jnp.maximum(peak, lse_in[it, k])
        total = jnp.exp(lse_out[it] - peak)
        for k in range(1, members):
            total += jnp.exp(lse_in[it, k] - peak)
        shift = -(peak + jnp.log(total))
        for t in range(tiles):
            lanes = slice(t * LANES, (t + 1) * LANES)
            row_shift[0:1, lanes] = jnp.where(
                live[t : t + 1, :] > 0.5, shift[t : t + 1, :], -jnp.inf
            )
        for c in range(noise_count // row_chunk):
            span = slice(c * row_chunk, (c + 1) * row_chunk)
            scores = cost[span, :] + row_shift[0:1, :]
            peak = jnp.max(scores, axis=1, keepdims=True)
            exponent = jnp.exp(scores - peak)
            total = jnp.sum(exponent, axis=1, keepdims=True)
            if it < ITERS - 1:
                col_shift[span, :] = jnp.broadcast_to(-(peak + jnp.log(total)), (row_chunk, LANES))
            else:
                weights[span, :] = (exponent / total).astype(jnp.bfloat16)
        for copy in lse_copies:
            copy.wait_send()


def pair(slots, counts, noise, sent, collective_id):
    members = SIDE * SIDE
    capacity = -(-sent // (3 * LANES)) * 3 * LANES if sent < members * ROWS_DEV else sent
    noise_count, width = noise.shape
    tiles = capacity // LANES
    part_width = width // members
    dma = pltpu.SemaphoreType.DMA
    vmem = pl.BlockSpec(memory_space=pltpu.VMEM)
    return pl.pallas_call(
        functools.partial(pairing_kernel, width, sent),
        out_shape=(
            jax.ShapeDtypeStruct((members, 2, capacity, LANES), jnp.bfloat16),
            jax.ShapeDtypeStruct((noise_count, capacity), jnp.bfloat16),
        ),
        in_specs=[vmem, vmem, pl.BlockSpec(memory_space=pl.ANY)],
        out_specs=(vmem, vmem),
        scratch_shapes=[
            pltpu.VMEM((noise_count, capacity), jnp.float32),
            pltpu.VMEM((noise_count, width), jnp.float32),
            pltpu.VMEM((members, noise_count, part_width), jnp.bfloat16),
            pltpu.VMEM((8, capacity), jnp.float32),
            pltpu.VMEM((tiles, LANES), jnp.float32),
            pltpu.VMEM((members, LANES), jnp.float32),
            pltpu.VMEM((noise_count, LANES), jnp.float32),
            pltpu.VMEM((8, capacity), jnp.float32),
            pltpu.VMEM((ITERS, tiles, LANES), jnp.float32),
            pltpu.VMEM((ITERS, members, tiles, LANES), jnp.float32),
            dma((4,)),
            dma((2, 2, 2)),
            dma((2, 2, 2)),
            dma((2, 2, 5, 2)),
            dma((2, 2, 5, 2)),
            dma((ITERS, members)),
            dma((ITERS, members)),
        ],
        compiler_params=pltpu.CompilerParams(
            collective_id=collective_id, has_side_effects=True, vmem_limit_bytes=30 * 1024 * 1024
        ),
    )(slots, counts, noise)


def routing_kernel(
    dest_hbm,
    loaded_hbm,
    slots_ref,
    count_ref,
    dest_ref,
    loaded_ref,
    packed,
    landed,
    tally,
    tally_bucket,
    tally_member,
    load_sem,
    bucket_send,
    bucket_recv,
    member_send,
    member_recv,
    tally_send,
    tally_recv,
):
    groups, members = BUCKETS, SIDE * SIDE
    loaded, width = loaded_ref.shape
    part_width = width // members
    block = ROWS_DEV // groups
    my_bucket, me = lax.axis_index("bucket"), lax.axis_index("member")
    bucket_peers = [(my_bucket + k) % groups for k in range(groups)]
    member_peers = [(me + k) % members for k in range(members)]

    dest_copy = pltpu.make_async_copy(dest_hbm, dest_ref, load_sem.at[0])
    dest_copy.start()
    load_copy = pltpu.make_async_copy(loaded_hbm, loaded_ref, load_sem.at[1])
    load_copy.start()
    barrier = pltpu.get_barrier_semaphore()
    for peer in bucket_peers[1:]:
        pl.semaphore_signal(barrier, inc=1, device_id={"bucket": peer}, device_id_type=MESH)
    for peer in member_peers[1:]:
        pl.semaphore_signal(barrier, inc=1, device_id={"member": peer}, device_id_type=MESH)

    dest_copy.wait()
    dest = dest_ref[...]
    hits = (lax.broadcasted_iota(jnp.int32, (groups, loaded), 0) == dest).astype(jnp.float32)
    up_to = (
        lax.broadcasted_iota(jnp.int32, (loaded, loaded), 0)
        <= lax.broadcasted_iota(jnp.int32, (loaded, loaded), 1)
    ).astype(jnp.bfloat16)
    ranks = jnp.dot(hits.astype(jnp.bfloat16), up_to, preferred_element_type=jnp.float32)
    place = jnp.sum(hits * (ranks - 1.0), axis=0, keepdims=True).astype(jnp.int32) + dest * block
    pick = lax.broadcasted_iota(jnp.int32, (ROWS_DEV, loaded), 0) == place
    pick = pick.astype(jnp.float32)
    fill = EMPTY * (1.0 - jnp.sum(pick, axis=1, keepdims=True))
    pick = pick.astype(jnp.bfloat16)
    tally[0] = jnp.broadcast_to(jnp.sum(hits, axis=1, keepdims=True), tally.shape[1:])
    load_copy.wait()

    def pack(k):
        start = pl.multiple_of(member_peers[k] * part_width, part_width)
        panel = loaded_ref[:, pl.ds(start, part_width)].astype(jnp.bfloat16)
        sorted_panel = jnp.dot(pick, panel, preferred_element_type=jnp.float32) + fill
        sorted_panel = sorted_panel.astype(jnp.bfloat16)
        for part in range(2):
            packed[part, k] = sorted_panel[:, part * LANES : (part + 1) * LANES]

    def block_of(bucket):
        return pl.ds(pl.multiple_of(bucket * block, block), block)

    def to_bucket(stage, k, source, target):
        copy = pltpu.make_async_remote_copy(
            src_ref=source.at[:, block_of(bucket_peers[k])],
            dst_ref=target.at[:, block_of(my_bucket)],
            send_sem=bucket_send.at[stage, k],
            recv_sem=bucket_recv.at[stage, k],
            device_id={"bucket": bucket_peers[k]},
            device_id_type=MESH,
        )
        copy.start()
        return copy

    def to_member(stage, k, source, target):
        copy = pltpu.make_async_remote_copy(
            src_ref=source,
            dst_ref=target,
            send_sem=member_send.at[stage, k],
            recv_sem=member_recv.at[stage, k],
            device_id={"member": member_peers[k]},
            device_id_type=MESH,
        )
        copy.start()
        return copy

    def tell(stage, k, target, axis, peer):
        copy = pltpu.make_async_remote_copy(
            src_ref=tally.at[stage],
            dst_ref=target.at[k],
            send_sem=tally_send.at[stage, k],
            recv_sem=tally_recv.at[stage, k],
            device_id={axis: peer},
            device_id_type=MESH,
        )
        copy.start()
        return copy

    for k in range(members):
        pack(k)
    pl.semaphore_wait(barrier, groups + members - 2)
    bucket_tally = [tell(0, k, tally_bucket, "bucket", bucket_peers[k]) for k in range(1, groups)]
    first_bucket, first_member = [], []
    for k in range(1, members):
        if k < groups:
            first_bucket.append(to_bucket(0, k, packed.at[0], landed.at[0]))
        first_member.append(to_member(0, k, packed.at[1, k], landed.at[1, me]))
    landed[0, :, block_of(my_bucket), :] = packed[0, :, block_of(my_bucket), :]
    landed[1, me] = packed[1, 0]

    for copy in first_bucket:
        copy.wait_recv()
    second_member = [
        to_member(1, k, landed.at[0, k], slots_ref.at[0, me]) for k in range(1, members)
    ]
    slots_ref[0, me] = landed[0, 0]
    for copy in first_member:
        copy.wait_recv()
    second_bucket = [to_bucket(1, k, landed.at[1], slots_ref.at[1]) for k in range(1, groups)]
    slots_ref[1, :, block_of(my_bucket), :] = landed[1, :, block_of(my_bucket), :]

    total = tally[0]
    for k in range(1, groups):
        bucket_tally[k - 1].wait_recv()
        total += tally_bucket[k]
    tally[1] = total
    member_tally = [tell(1, k, tally_member, "member", member_peers[k]) for k in range(1, members)]
    for k in range(1, members):
        member_tally[k - 1].wait_recv()
        total += tally_member[k]
    count_ref[...] = total
    for copy in second_member + second_bucket:
        copy.wait_recv()
    for copy in (
        first_bucket + first_member + second_member + second_bucket + bucket_tally + member_tally
    ):
        copy.wait_send()


def route(dest_bucket, loader_rows):
    members = SIDE * SIDE
    loaded, width = loader_rows.shape
    dma = pltpu.SemaphoreType.DMA
    vmem = pl.BlockSpec(memory_space=pltpu.VMEM)
    anywhere = pl.BlockSpec(memory_space=pl.ANY)
    return pl.pallas_call(
        routing_kernel,
        out_shape=(
            jax.ShapeDtypeStruct((2, members, ROWS_DEV, LANES), jnp.bfloat16),
            jax.ShapeDtypeStruct((BUCKETS, LANES), jnp.float32),
        ),
        in_specs=[anywhere, anywhere],
        out_specs=(vmem, vmem),
        scratch_shapes=[
            pltpu.VMEM((1, loaded), jnp.int32),
            pltpu.VMEM((loaded, width), jnp.float32),
            pltpu.VMEM((2, members, ROWS_DEV, LANES), jnp.bfloat16),
            pltpu.VMEM((2, members, ROWS_DEV, LANES), jnp.bfloat16),
            pltpu.VMEM((2, BUCKETS, LANES), jnp.float32),
            pltpu.VMEM((BUCKETS, BUCKETS, LANES), jnp.float32),
            pltpu.VMEM((members, BUCKETS, LANES), jnp.float32),
            dma((2,)),
            dma((2, BUCKETS)),
            dma((2, BUCKETS)),
            dma((2, members)),
            dma((2, members)),
            dma((2, members)),
            dma((2, members)),
        ],
        compiler_params=pltpu.CompilerParams(
            collective_id=1, has_side_effects=True, vmem_limit_bytes=16 * 1024 * 1024
        ),
    )(dest_bucket.reshape(1, -1), loader_rows)


def targets_kernel(rows_ref, weights_ref, out_ref):
    q = pl.program_id(0)
    panel = jnp.concatenate([rows_ref[q, 0], rows_ref[q, 1]], axis=1)
    out_ref[...] = jnp.dot(weights_ref[...], panel, preferred_element_type=jnp.float32)


def multiply(rows, weights):
    members, _, capacity, _ = rows.shape
    noise_count = weights.shape[0]
    width = members * 2 * LANES
    vmem = pl.BlockSpec(memory_space=pltpu.VMEM)
    return pl.pallas_call(
        targets_kernel,
        out_shape=jax.ShapeDtypeStruct((noise_count, width), jnp.float32),
        grid=(members,),
        in_specs=[vmem, vmem],
        out_specs=pl.BlockSpec((noise_count, 2 * LANES), lambda q: (0, q)),
        compiler_params=pltpu.CompilerParams(vmem_limit_bytes=24 * 1024 * 1024),
    )(rows, weights)


def body(loader_rows, dest_bucket, dest_slot, noise):
    slots, counts = route(dest_bucket, loader_rows)

    def all_slots(slots, counts, noise):
        return multiply(*pair(slots, counts, noise, slots.shape[1] * ROWS_DEV, 2))

    def live_first(slots, counts, noise):
        return multiply(*pair(slots, counts, noise, FAST_ROWS, 0))

    return lax.cond(jnp.all(counts <= FAST_ROWS), live_first, all_slots, slots, counts, noise)


def solution(mesh):
    return jax.shard_map(
        body,
        mesh=mesh,
        in_specs=(
            P(("bucket", "member"), None),
            P(("bucket", "member")),
            P(("bucket", "member")),
            P(("bucket", "member"), None),
        ),
        out_specs=P(("bucket", "member"), None),
        check_vma=False,
    )
```

```python
import functools
import math

import jax
import jax.numpy as jnp
from jax import lax
from jax.experimental import pallas as pl
from jax.experimental.pallas import tpu as pltpu
from jax.sharding import PartitionSpec as P

ROWS_DEV = 128
ITERS = 4
SIDE = 4
BUCKETS = 8
FAST_ROWS = 1120
LANES = 128
EMPTY = 16384.0
MESH = pl.DeviceIdType.MESH
CONTRACT_LAST = (((1,), (1,)), ((), ()))


def solve(width, sent, eager, prepare, extra, noise_norm_of, rows, weights, scratch):
    (cost, noise_rows, row_norm, live, col_shift, row_shift, lse_out, lse_in,
     first_send, first_recv, second_send, second_recv, lse_send, lse_recv) = scratch
    members = SIDE * SIDE
    capacity = rows.shape[2]
    noise_count = cost.shape[0]
    tiles = capacity // LANES
    scale = 1.0 / (width * (0.64 / math.sqrt(width)))
    me = lax.axis_index("member")
    my_z, my_x = me // SIDE, me % SIDE

    def member_at(part, first, second):
        along_x, along_z = (first, second) if part == 0 else (second, first)
        return ((my_z + along_z + SIDE) % SIDE) * SIDE + (my_x + along_x + SIDE) % SIDE

    def front(count):
        return -(-count // 32) * 16

    half = front(sent)
    units = [(0, 0, sent), (-1, 0, sent), (1, 0, sent), (2, 0, half), (2, half, sent - half)]
    ways = (1, -1)
    pending = {}

    def side(start, count, d):
        middle = front(count)
        return (start, middle) if d == 0 else (start + middle, count - middle)

    def send(label, part, owner, span, neighbour, sems):
        piece = rows.at[owner, part, pl.ds(*span)]
        copy = pltpu.make_async_remote_copy(
            src_ref=piece,
            dst_ref=piece,
            send_sem=sems[0],
            recv_sem=sems[1],
            device_id={"member": neighbour},
            device_id_type=MESH,
        )
        copy.start()
        pending[label] = copy

    def first_hop(part, d):
        sems = (first_send.at[part, 0, d], first_recv.at[part, 0, d])
        send(("f1", part, d), part, me, (0, sent), member_at(part, ways[d], 0), sems)

    def first_forward(part, d):
        sems = (first_send.at[part, 1, d], first_recv.at[part, 1, d])
        owner = member_at(part, -ways[d], 0)
        send(("f2", part, d), part, owner, side(0, sent, d), member_at(part, ways[d], 0), sems)

    def second_hop(part, u, d):
        first, start, count = units[u]
        sems = (second_send.at[part, 0, u, d], second_recv.at[part, 0, u, d])
        owner = me if u == 0 else member_at(part, first, 0)
        send(("g1", part, u, d), part, owner, (start, count), member_at(part, 0, ways[d]), sems)

    def second_forward(part, u, d):
        first, start, count = units[u]
        sems = (second_send.at[part, 1, u, d], second_recv.at[part, 1, u, d])
        owner = member_at(part, first, -ways[d])
        send(
            ("g2", part, u, d), part, owner, side(start, count, d), member_at(part, 0, ways[d]), sems
        )

    def arrive(label):
        pending[label].wait_recv()

    def add_slice(owner):
        if eager:
            add_panel(owner)

    def add_panel(owner):
        panel = jnp.concatenate([rows[owner, 0], rows[owner, 1]], axis=1)
        cost[...] += lax.dot_general(
            noise_rows[owner], panel, CONTRACT_LAST, preferred_element_type=jnp.float32
        )
        wide = panel.astype(jnp.float32)
        square = wide * wide
        high = square.astype(jnp.bfloat16)
        low = (square - high.astype(jnp.float32)).astype(jnp.bfloat16)
        ones = jnp.ones((8, panel.shape[1]), jnp.bfloat16)
        row_norm[...] += lax.dot_general(
            ones, high, CONTRACT_LAST, preferred_element_type=jnp.float32
        ) + lax.dot_general(ones, low, CONTRACT_LAST, preferred_element_type=jnp.float32)

    for part in range(2):
        prepare(part)
        for d in range(2):
            first_hop(part, d)
        for d in range(2):
            second_hop(part, 0, d)
    extra()
    cost[...] = jnp.zeros_like(cost)
    row_norm[...] = jnp.zeros_like(row_norm)
    noise_norm = noise_norm_of()
    add_slice(me)

    for part in range(2):
        for d in range(2):
            arrive(("f1", part, d))
            first_forward(part, d)
            u = 1 if d == 0 else 2
            for e in range(2):
                second_hop(part, u, e)
    for part in range(2):
        for d in range(2):
            arrive(("g1", part, 0, d))
            second_forward(part, 0, d)
    for step in ways:
        add_slice(member_at(0, step, 0))
        add_slice(member_at(0, 0, step))
    for d in range(2):
        for part in range(2):
            arrive(("f2", part, d))
            for e in range(2):
                second_hop(part, 3 + d, e)
    for u in (1, 2):
        for part in range(2):
            for d in range(2):
                arrive(("g1", part, u, d))
                second_forward(part, u, d)
    for step in ways:
        for other in ways:
            add_slice(member_at(0, step, other))
    for u in (3, 4):
        for part in range(2):
            for d in range(2):
                arrive(("g1", part, u, d))
                second_forward(part, u, d)
    for part in range(2):
        for d in range(2):
            arrive(("g2", part, 0, d))
    for part in range(2):
        add_slice(member_at(part, 2, 0))
    for u in (1, 2):
        for part in range(2):
            for d in range(2):
                arrive(("g2", part, u, d))
        for part in range(2):
            add_slice(member_at(part, units[u][0], 2))
    for u in (3, 4):
        for part in range(2):
            for d in range(2):
                arrive(("g2", part, u, d))
    add_slice(member_at(0, 2, 2))
    for copy in pending.values():
        copy.wait_send()

    if not eager:
        pl.loop(0, members)(add_panel)

    for t in range(tiles):
        lanes = slice(t * LANES, (t + 1) * LANES)
        cost[:, lanes] = (2.0 * cost[:, lanes] - row_norm[0:1, lanes] - noise_norm) * scale

    col_shift[...] = jnp.zeros_like(col_shift)
    row_chunk = 32
    for it in range(ITERS):
        for t in range(tiles):
            lanes = slice(t * LANES, (t + 1) * LANES)
            scores = cost[:, lanes] + col_shift[...]
            peak = jnp.max(scores, axis=0, keepdims=True)
            total = jnp.sum(jnp.exp(scores - peak), axis=0, keepdims=True)
            lse_out[it, t : t + 1, :] = peak + jnp.log(total)
        lse_copies = []
        for k in range(1, members):
            copy = pltpu.make_async_remote_copy(
                src_ref=lse_out.at[it],
                dst_ref=lse_in.at[it, k],
                send_sem=lse_send.at[it, k],
                recv_sem=lse_recv.at[it, k],
                device_id={"member": (me + k) % members},
                device_id_type=MESH,
            )
            copy.start()
            lse_copies.append(copy)
        for copy in lse_copies:
            copy.wait_recv()
        peak = lse_out[it]
        for k in range(1, members):
            peak = jnp.maximum(peak, lse_in[it, k])
        total = jnp.exp(lse_out[it] - peak)
        for k in range(1, members):
            total += jnp.exp(lse_in[it, k] - peak)
        shift = -(peak + jnp.log(total))
        for t in range(tiles):
            lanes = slice(t * LANES, (t + 1) * LANES)
            row_shift[0:1, lanes] = jnp.where(
                live[t : t + 1, :] > 0.5, shift[t : t + 1, :], -jnp.inf
            )
        for c in range(noise_count // row_chunk):
            span = slice(c * row_chunk, (c + 1) * row_chunk)
            scores = cost[span, :] + row_shift[0:1, :]
            peak = jnp.max(scores, axis=1, keepdims=True)
            exponent = jnp.exp(scores - peak)
            total = jnp.sum(exponent, axis=1, keepdims=True)
            if it < ITERS - 1:
                col_shift[span, :] = jnp.broadcast_to(-(peak + jnp.log(total)), (row_chunk, LANES))
            else:
                weights[span, :] = (exponent / total).astype(jnp.bfloat16)
        for copy in lse_copies:
            copy.wait_send()


def start_noise(noise_hbm, noise_wide, noise_sem):
    chunk = noise_wide.shape[1] // 4
    copies = []
    for k in range(4):
        columns = pl.ds(k * chunk, chunk)
        copy = pltpu.make_async_copy(
            noise_hbm.at[:, columns], noise_wide.at[:, columns], noise_sem.at[k]
        )
        copy.start()
        copies.append(copy)
    return copies


def round_noise(copies, noise_wide, noise_rows):
    noise_count, part_width = noise_rows.shape[1:]
    per_chunk = noise_rows.shape[0] // 4
    noise_norm = jnp.zeros((noise_count, 1), jnp.float32)
    for k in range(4):
        copies[k].wait()
        for s in range(per_chunk):
            q = k * per_chunk + s
            block = noise_wide[:, q * part_width : (q + 1) * part_width].astype(jnp.bfloat16)
            noise_rows[q] = block
            wide = block.astype(jnp.float32)
            noise_norm += jnp.sum(wide * wide, axis=1, keepdims=True)
    return noise_norm


def marked_live(slots_ref):
    marks = jnp.concatenate(
        [
            lax.dot_general(
                jnp.ones((8, LANES), jnp.bfloat16), slots_ref[0, t], CONTRACT_LAST,
                preferred_element_type=jnp.float32,
            )[0:1]
            for t in range(slots_ref.shape[1])
        ],
        axis=0,
    )
    return (marks < 0.5 * LANES * EMPTY).astype(jnp.float32)


def all_slots_kernel(width, slots_ref, noise_hbm, rows, weights, noise_wide, noise_sem, *scratch):
    noise_rows, live = scratch[1], scratch[3]
    members = SIDE * SIDE
    me = lax.axis_index("member")
    noise_copies = start_noise(noise_hbm, noise_wide, noise_sem)
    barrier = pltpu.get_barrier_semaphore()
    for k in range(1, members):
        pl.semaphore_signal(
            barrier, inc=1, device_id={"member": (me + k) % members}, device_id_type=MESH
        )
    live[...] = marked_live(slots_ref)
    for part in range(2):
        for t in range(members):
            block = slots_ref[part, t].astype(jnp.float32)
            block = jnp.where(block < 0.5 * EMPTY, block, 0.0)
            rows[me, part, t * ROWS_DEV : (t + 1) * ROWS_DEV, :] = block.astype(jnp.bfloat16)
    pl.semaphore_wait(barrier, members - 1)
    solve(
        width, rows.shape[2], False, lambda part: None, lambda: None,
        lambda: round_noise(noise_copies, noise_wide, noise_rows), rows, weights, scratch,
    )


def live_rows_kernel(
    width,
    sent,
    dest_hbm,
    loaded_hbm,
    noise_hbm,
    rows,
    weights,
    slots_ref,
    count_ref,
    dest_ref,
    loaded_ref,
    packed,
    landed,
    tally,
    tally_bucket,
    tally_member,
    load_sem,
    bucket_send,
    bucket_recv,
    member_send,
    member_recv,
    tally_send,
    tally_recv,
    position,
    choose,
    noise_wide,
    noise_sem,
    *scratch,
):
    noise_rows, live = scratch[1], scratch[3]
    groups, members = BUCKETS, SIDE * SIDE
    loaded = loaded_ref.shape[0]
    capacity = rows.shape[2]
    tiles = capacity // LANES
    part_width = width // members
    block = ROWS_DEV // groups
    my_bucket, me = lax.axis_index("bucket"), lax.axis_index("member")
    bucket_peers = [(my_bucket + k) % groups for k in range(groups)]
    member_peers = [(me + k) % members for k in range(members)]

    dest_copy = pltpu.make_async_copy(dest_hbm, dest_ref, load_sem.at[0])
    dest_copy.start()
    load_copy = pltpu.make_async_copy(loaded_hbm, loaded_ref, load_sem.at[1])
    load_copy.start()
    noise_copies = start_noise(noise_hbm, noise_wide, noise_sem)
    barrier = pltpu.get_barrier_semaphore()
    for peer in bucket_peers[1:]:
        pl.semaphore_signal(barrier, inc=1, device_id={"bucket": peer}, device_id_type=MESH)
    for peer in member_peers[1:]:
        pl.semaphore_signal(barrier, inc=1, device_id={"member": peer}, device_id_type=MESH)

    dest_copy.wait()
    dest = dest_ref[...]
    hits = (lax.broadcasted_iota(jnp.int32, (groups, loaded), 0) == dest).astype(jnp.float32)
    up_to = (
        lax.broadcasted_iota(jnp.int32, (loaded, loaded), 0)
        <= lax.broadcasted_iota(jnp.int32, (loaded, loaded), 1)
    ).astype(jnp.bfloat16)
    ranks = jnp.dot(hits.astype(jnp.bfloat16), up_to, preferred_element_type=jnp.float32)
    place = jnp.sum(hits * (ranks - 1.0), axis=0, keepdims=True).astype(jnp.int32) + dest * block
    pick = lax.broadcasted_iota(jnp.int32, (ROWS_DEV, loaded), 0) == place
    pick = pick.astype(jnp.float32)
    fill = EMPTY * (1.0 - jnp.sum(pick, axis=1, keepdims=True))
    pick = pick.astype(jnp.bfloat16)
    tally[0] = jnp.broadcast_to(jnp.sum(hits, axis=1, keepdims=True), tally.shape[1:])
    load_copy.wait()

    def pack(k):
        start = pl.multiple_of(member_peers[k] * part_width, part_width)
        panel = loaded_ref[:, pl.ds(start, part_width)].astype(jnp.bfloat16)
        sorted_panel = jnp.dot(pick, panel, preferred_element_type=jnp.float32) + fill
        sorted_panel = sorted_panel.astype(jnp.bfloat16)
        for part in range(2):
            packed[part, k] = sorted_panel[:, part * LANES : (part + 1) * LANES]

    def block_of(bucket):
        return pl.ds(pl.multiple_of(bucket * block, block), block)

    def to_bucket(stage, k, source, target):
        copy = pltpu.make_async_remote_copy(
            src_ref=source.at[:, block_of(bucket_peers[k])],
            dst_ref=target.at[:, block_of(my_bucket)],
            send_sem=bucket_send.at[stage, k],
            recv_sem=bucket_recv.at[stage, k],
            device_id={"bucket": bucket_peers[k]},
            device_id_type=MESH,
        )
        copy.start()
        return copy

    def to_member(stage, k, source, target):
        copy = pltpu.make_async_remote_copy(
            src_ref=source,
            dst_ref=target,
            send_sem=member_send.at[stage, k],
            recv_sem=member_recv.at[stage, k],
            device_id={"member": member_peers[k]},
            device_id_type=MESH,
        )
        copy.start()
        return copy

    def tell(stage, k, target, axis, peer):
        copy = pltpu.make_async_remote_copy(
            src_ref=tally.at[stage],
            dst_ref=target.at[k],
            send_sem=tally_send.at[stage, k],
            recv_sem=tally_recv.at[stage, k],
            device_id={axis: peer},
            device_id_type=MESH,
        )
        copy.start()
        return copy

    for k in range(members):
        pack(k)
    pl.semaphore_wait(barrier, groups + members - 2)
    bucket_tally = [tell(0, k, tally_bucket, "bucket", bucket_peers[k]) for k in range(1, groups)]
    first_bucket, first_member = [], []
    for k in range(1, members):
        if k < groups:
            first_bucket.append(to_bucket(0, k, packed.at[0], landed.at[0]))
        first_member.append(to_member(0, k, packed.at[1, k], landed.at[1, me]))
    landed[0, :, block_of(my_bucket), :] = packed[0, :, block_of(my_bucket), :]
    landed[1, me] = packed[1, 0]

    noise_norm = round_noise(noise_copies, noise_wide, noise_rows)
    if sent < capacity:
        blank = jnp.zeros((capacity - sent, LANES), jnp.bfloat16)
        for q in range(members):
            for part in range(2):
                rows[q, part, sent:capacity, :] = blank

    for copy in first_bucket:
        copy.wait_recv()
    second_member = [
        to_member(1, k, landed.at[0, k], slots_ref.at[0, me]) for k in range(1, members)
    ]
    slots_ref[0, me] = landed[0, 0]
    for copy in first_member:
        copy.wait_recv()
    second_bucket = [to_bucket(1, k, landed.at[1], slots_ref.at[1]) for k in range(1, groups)]
    slots_ref[1, :, block_of(my_bucket), :] = landed[1, :, block_of(my_bucket), :]
    total = tally[0]
    for k in range(1, groups):
        bucket_tally[k - 1].wait_recv()
        total += tally_bucket[k]
    tally[1] = total
    member_tally = [tell(1, k, tally_member, "member", member_peers[k]) for k in range(1, members)]

    def find_positions():
        alive = marked_live(slots_ref)
        before = (
            lax.broadcasted_iota(jnp.int32, (LANES, LANES), 0)
            <= lax.broadcasted_iota(jnp.int32, (LANES, LANES), 1)
        ).astype(jnp.bfloat16)
        inside = jnp.dot(alive.astype(jnp.bfloat16), before, preferred_element_type=jnp.float32)
        per_member = jnp.broadcast_to(inside[:, LANES - 1 : LANES], (members, LANES))
        earlier = (
            lax.broadcasted_iota(jnp.int32, (members, members), 0)
            > lax.broadcasted_iota(jnp.int32, (members, members), 1)
        ).astype(jnp.bfloat16)
        offset = jnp.dot(
            earlier, per_member.astype(jnp.bfloat16), preferred_element_type=jnp.float32
        )
        position[...] = jnp.where(alive > 0.5, inside + offset - 1.0, -1.0)
        held = jnp.sum(per_member, axis=0, keepdims=True)
        place = lax.broadcasted_iota(jnp.int32, (tiles, LANES), 0) * LANES
        place += lax.broadcasted_iota(jnp.int32, (tiles, LANES), 1)
        live[...] = (place.astype(jnp.float32) < held).astype(jnp.float32)

    step = capacity // 3

    def prepare(part):
        for copy in second_bucket if part else second_member:
            copy.wait_recv()
        if part == 0:
            find_positions()

        @pl.loop(0, 3)
        def _(c):
            start = pl.multiple_of(c * step, LANES)
            span = pl.ds(start, step)
            if part == 0:
                target = lax.broadcasted_iota(jnp.int32, (step, LANES), 0) + start
                target = target.astype(jnp.float32)
                for t in range(members):
                    choose[span, t * LANES : (t + 1) * LANES] = (
                        target == position[t : t + 1, :]
                    ).astype(jnp.bfloat16)
            rows[me, part, span, :] = jnp.dot(
                choose[span, :],
                slots_ref[part].reshape(members * ROWS_DEV, LANES),
                preferred_element_type=jnp.float32,
            ).astype(jnp.bfloat16)

    def finish_count():
        total = tally[1]
        for k in range(1, members):
            member_tally[k - 1].wait_recv()
            total += tally_member[k]
        count_ref[...] = total

    solve(width, sent, True, prepare, finish_count, lambda: noise_norm, rows, weights, scratch)
    for copy in (
        first_bucket + first_member + second_member + second_bucket + bucket_tally + member_tally
    ):
        copy.wait_send()


def solve_scratch(noise_count, capacity, width):
    members = SIDE * SIDE
    tiles = capacity // LANES
    dma = pltpu.SemaphoreType.DMA
    return [
        pltpu.VMEM((noise_count, width), jnp.float32),
        dma((4,)),
        pltpu.VMEM((noise_count, capacity), jnp.float32),
        pltpu.VMEM((members, noise_count, width // members), jnp.bfloat16),
        pltpu.VMEM((8, capacity), jnp.float32),
        pltpu.VMEM((tiles, LANES), jnp.float32),
        pltpu.VMEM((noise_count, LANES), jnp.float32),
        pltpu.VMEM((8, capacity), jnp.float32),
        pltpu.VMEM((ITERS, tiles, LANES), jnp.float32),
        pltpu.VMEM((ITERS, members, tiles, LANES), jnp.float32),
        dma((2, 2, 2)),
        dma((2, 2, 2)),
        dma((2, 2, 5, 2)),
        dma((2, 2, 5, 2)),
        dma((ITERS, members)),
        dma((ITERS, members)),
    ]


IN_VMEM = pl.BlockSpec(memory_space=pltpu.VMEM)
IN_HBM = pl.BlockSpec(memory_space=pltpu.HBM)


def in_hbm(array):
    return pltpu.with_memory_space_constraint(array, pltpu.HBM)


def pair_live_rows(dest_bucket, loader_rows, noise):
    members = SIDE * SIDE
    capacity = -(-FAST_ROWS // (3 * LANES)) * 3 * LANES
    loaded, width = loader_rows.shape
    noise_count = noise.shape[0]
    dma = pltpu.SemaphoreType.DMA
    return pl.pallas_call(
        functools.partial(live_rows_kernel, width, FAST_ROWS),
        out_shape=(
            jax.ShapeDtypeStruct((members, 2, capacity, LANES), jnp.bfloat16),
            jax.ShapeDtypeStruct((noise_count, capacity), jnp.bfloat16),
            jax.ShapeDtypeStruct((2, members, ROWS_DEV, LANES), jnp.bfloat16),
            jax.ShapeDtypeStruct((BUCKETS, LANES), jnp.float32),
        ),
        in_specs=[IN_HBM, IN_HBM, IN_HBM],
        out_specs=(IN_VMEM, IN_VMEM, IN_VMEM, IN_VMEM),
        scratch_shapes=[
            pltpu.VMEM((1, loaded), jnp.int32),
            pltpu.VMEM((loaded, width), jnp.float32),
            pltpu.VMEM((2, members, ROWS_DEV, LANES), jnp.bfloat16),
            pltpu.VMEM((2, members, ROWS_DEV, LANES), jnp.bfloat16),
            pltpu.VMEM((2, BUCKETS, LANES), jnp.float32),
            pltpu.VMEM((BUCKETS, BUCKETS, LANES), jnp.float32),
            pltpu.VMEM((members, BUCKETS, LANES), jnp.float32),
            dma((2,)),
            dma((2, BUCKETS)),
            dma((2, BUCKETS)),
            dma((2, members)),
            dma((2, members)),
            dma((2, members)),
            dma((2, members)),
            pltpu.VMEM((members, LANES), jnp.float32),
            pltpu.VMEM((capacity, members * ROWS_DEV), jnp.bfloat16),
            *solve_scratch(noise_count, capacity, width),
        ],
        compiler_params=pltpu.CompilerParams(
            collective_id=0, has_side_effects=True, vmem_limit_bytes=20 * 1024 * 1024
        ),
    )(*[in_hbm(array) for array in (dest_bucket.reshape(1, -1), loader_rows, noise)])


def pair_all_slots(slots, noise):
    members = SIDE * SIDE
    capacity = members * ROWS_DEV
    noise_count, width = noise.shape
    return pl.pallas_call(
        functools.partial(all_slots_kernel, width),
        out_shape=(
            jax.ShapeDtypeStruct((members, 2, capacity, LANES), jnp.bfloat16),
            jax.ShapeDtypeStruct((noise_count, capacity), jnp.bfloat16),
        ),
        in_specs=[IN_VMEM, IN_HBM],
        out_specs=(IN_VMEM, IN_VMEM),
        scratch_shapes=solve_scratch(noise_count, capacity, width),
        compiler_params=pltpu.CompilerParams(
            collective_id=1, has_side_effects=True, vmem_limit_bytes=14 * 1024 * 1024
        ),
    )(slots, noise)


def targets_kernel(rows_ref, weights_ref, out_hbm, made, sem):
    members = rows_ref.shape[0]
    part_width = 2 * LANES

    def out_copy(q):
        start = pl.multiple_of(q * part_width, part_width)
        return pltpu.make_async_copy(
            made.at[q], out_hbm.at[:, pl.ds(start, part_width)], sem.at[q]
        )

    @pl.loop(0, members)
    def _(q):
        panel = jnp.concatenate([rows_ref[q, 0], rows_ref[q, 1]], axis=1)
        made[q] = jnp.dot(weights_ref[...], panel, preferred_element_type=jnp.float32)
        out_copy(q).start()

    @pl.loop(0, members)
    def _(q):
        out_copy(q).wait()


def multiply(rows, weights):
    members = rows.shape[0]
    noise_count = weights.shape[0]
    width = members * 2 * LANES
    return pl.pallas_call(
        targets_kernel,
        out_shape=pltpu.HBM((noise_count, width), jnp.float32),
        in_specs=[IN_VMEM, IN_VMEM],
        out_specs=IN_HBM,
        scratch_shapes=[
            pltpu.VMEM((members, noise_count, 2 * LANES), jnp.float32),
            pltpu.SemaphoreType.DMA((members,)),
        ],
        compiler_params=pltpu.CompilerParams(vmem_limit_bytes=12 * 1024 * 1024),
    )(rows, weights)


def body(loader_rows, dest_bucket, dest_slot, noise):
    rows, weights, slots, counts = pair_live_rows(dest_bucket, loader_rows, noise)

    targets = multiply(rows, weights)

    def with_all_slots(state):
        return jnp.zeros((), jnp.bool_), multiply(*pair_all_slots(slots, noise))

    overfull = jnp.any(counts > FAST_ROWS)
    return lax.while_loop(lambda state: state[0], with_all_slots, (overfull, targets))[1]


def solution(mesh):
    return jax.shard_map(
        body,
        mesh=mesh,
        in_specs=(
            P(("bucket", "member"), None),
            P(("bucket", "member")),
            P(("bucket", "member")),
            P(("bucket", "member"), None),
        ),
        out_specs=P(("bucket", "member"), None),
        check_vma=False,
    )
```

```python
import functools
import math

import jax
import jax.numpy as jnp
from jax import lax
from jax.experimental import pallas as pl
from jax.experimental.pallas import tpu as pltpu
from jax.sharding import PartitionSpec as P

ROWS_DEV = 128
ITERS = 4
SIDE = 4
BUCKETS = 8
FAST_ROWS = 1104
LANES = 128
EMPTY = 16384.0
MESH = pl.DeviceIdType.MESH
CONTRACT_LAST = (((1,), (1,)), ((), ()))


def solve(width, sent, eager, prepare, extra, noise_norm_of, rows, weights, scratch):
    (cost, noise_rows, row_norm, live, col_shift, row_shift, lse_out, lse_in,
     first_send, first_recv, second_send, second_recv, lse_send, lse_recv) = scratch
    members = SIDE * SIDE
    capacity = rows.shape[2]
    noise_count = cost.shape[0]
    tiles = capacity // LANES
    scale = 1.0 / (width * (0.64 / math.sqrt(width)))
    me = lax.axis_index("member")
    my_z, my_x = me // SIDE, me % SIDE

    def member_at(part, first, second):
        along_x, along_z = (first, second) if part == 0 else (second, first)
        return ((my_z + along_z + SIDE) % SIDE) * SIDE + (my_x + along_x + SIDE) % SIDE

    def front(count):
        return -(-count // 32) * 16

    half = front(sent)
    units = [(0, 0, sent), (-1, 0, sent), (1, 0, sent), (2, 0, half), (2, half, sent - half)]
    ways = (1, -1)
    pending = {}

    def side(start, count, d):
        middle = front(count)
        return (start, middle) if d == 0 else (start + middle, count - middle)

    def send(label, part, owner, span, neighbour, sems):
        piece = rows.at[owner, part, pl.ds(*span)]
        copy = pltpu.make_async_remote_copy(
            src_ref=piece,
            dst_ref=piece,
            send_sem=sems[0],
            recv_sem=sems[1],
            device_id={"member": neighbour},
            device_id_type=MESH,
        )
        copy.start()
        pending[label] = copy

    def first_hop(part, d):
        sems = (first_send.at[part, 0, d], first_recv.at[part, 0, d])
        send(("f1", part, d), part, me, (0, sent), member_at(part, ways[d], 0), sems)

    def first_forward(part, d):
        sems = (first_send.at[part, 1, d], first_recv.at[part, 1, d])
        owner = member_at(part, -ways[d], 0)
        send(("f2", part, d), part, owner, side(0, sent, d), member_at(part, ways[d], 0), sems)

    def second_hop(part, u, d):
        first, start, count = units[u]
        sems = (second_send.at[part, 0, u, d], second_recv.at[part, 0, u, d])
        owner = me if u == 0 else member_at(part, first, 0)
        send(("g1", part, u, d), part, owner, (start, count), member_at(part, 0, ways[d]), sems)

    def second_forward(part, u, d):
        first, start, count = units[u]
        sems = (second_send.at[part, 1, u, d], second_recv.at[part, 1, u, d])
        owner = member_at(part, first, -ways[d])
        send(
            ("g2", part, u, d), part, owner, side(start, count, d), member_at(part, 0, ways[d]), sems
        )

    def arrive(label):
        pending[label].wait_recv()

    def add_slice(owner):
        if eager:
            add_panel(owner)

    def add_panel(owner):
        panel = jnp.concatenate([rows[owner, 0], rows[owner, 1]], axis=1)
        cost[...] += lax.dot_general(
            noise_rows[owner], panel, CONTRACT_LAST, preferred_element_type=jnp.float32
        )
        wide = panel.astype(jnp.float32)
        square = wide * wide
        high = square.astype(jnp.bfloat16)
        low = (square - high.astype(jnp.float32)).astype(jnp.bfloat16)
        ones = jnp.ones((8, panel.shape[1]), jnp.bfloat16)
        row_norm[...] += lax.dot_general(
            ones, high, CONTRACT_LAST, preferred_element_type=jnp.float32
        ) + lax.dot_general(ones, low, CONTRACT_LAST, preferred_element_type=jnp.float32)

    for part in range(2):
        prepare(part)
        for d in range(2):
            first_hop(part, d)
        for d in range(2):
            second_hop(part, 0, d)
    extra()
    cost[...] = jnp.zeros_like(cost)
    row_norm[...] = jnp.zeros_like(row_norm)
    noise_norm = noise_norm_of()
    add_slice(me)

    for part in range(2):
        for d in range(2):
            arrive(("f1", part, d))
            first_forward(part, d)
            u = 1 if d == 0 else 2
            for e in range(2):
                second_hop(part, u, e)
    for part in range(2):
        for d in range(2):
            arrive(("g1", part, 0, d))
            second_forward(part, 0, d)
    for step in ways:
        add_slice(member_at(0, step, 0))
        add_slice(member_at(0, 0, step))
    for d in range(2):
        for part in range(2):
            arrive(("f2", part, d))
            for e in range(2):
                second_hop(part, 3 + d, e)
    for u in (1, 2):
        for part in range(2):
            for d in range(2):
                arrive(("g1", part, u, d))
                second_forward(part, u, d)
    for step in ways:
        for other in ways:
            add_slice(member_at(0, step, other))
    for u in (3, 4):
        for part in range(2):
            for d in range(2):
                arrive(("g1", part, u, d))
                second_forward(part, u, d)
    for part in range(2):
        for d in range(2):
            arrive(("g2", part, 0, d))
    for part in range(2):
        add_slice(member_at(part, 2, 0))
    for u in (1, 2):
        for part in range(2):
            for d in range(2):
                arrive(("g2", part, u, d))
        for part in range(2):
            add_slice(member_at(part, units[u][0], 2))
    for u in (3, 4):
        for part in range(2):
            for d in range(2):
                arrive(("g2", part, u, d))
    add_slice(member_at(0, 2, 2))
    for copy in pending.values():
        copy.wait_send()

    if not eager:
        pl.loop(0, members)(add_panel)

    for t in range(tiles):
        lanes = slice(t * LANES, (t + 1) * LANES)
        cost[:, lanes] = (2.0 * cost[:, lanes] - row_norm[0:1, lanes] - noise_norm) * scale

    col_shift[...] = jnp.zeros_like(col_shift)
    row_chunk = 32
    for it in range(ITERS):
        for t in range(tiles):
            lanes = slice(t * LANES, (t + 1) * LANES)
            scores = cost[:, lanes] + col_shift[...]
            peak = jnp.max(scores, axis=0, keepdims=True)
            total = jnp.sum(jnp.exp(scores - peak), axis=0, keepdims=True)
            lse_out[it, t : t + 1, :] = peak + jnp.log(total)
        lse_copies = []
        for k in range(1, members):
            copy = pltpu.make_async_remote_copy(
                src_ref=lse_out.at[it],
                dst_ref=lse_in.at[it, k],
                send_sem=lse_send.at[it, k],
                recv_sem=lse_recv.at[it, k],
                device_id={"member": (me + k) % members},
                device_id_type=MESH,
            )
            copy.start()
            lse_copies.append(copy)
        for copy in lse_copies:
            copy.wait_recv()
        peak = lse_out[it]
        for k in range(1, members):
            peak = jnp.maximum(peak, lse_in[it, k])
        total = jnp.exp(lse_out[it] - peak)
        for k in range(1, members):
            total += jnp.exp(lse_in[it, k] - peak)
        shift = -(peak + jnp.log(total))
        for t in range(tiles):
            lanes = slice(t * LANES, (t + 1) * LANES)
            row_shift[0:1, lanes] = jnp.where(
                live[t : t + 1, :] > 0.5, shift[t : t + 1, :], -jnp.inf
            )
        for c in range(noise_count // row_chunk):
            span = slice(c * row_chunk, (c + 1) * row_chunk)
            scores = cost[span, :] + row_shift[0:1, :]
            peak = jnp.max(scores, axis=1, keepdims=True)
            exponent = jnp.exp(scores - peak)
            total = jnp.sum(exponent, axis=1, keepdims=True)
            if it < ITERS - 1:
                col_shift[span, :] = jnp.broadcast_to(-(peak + jnp.log(total)), (row_chunk, LANES))
            else:
                weights[span, :] = (exponent / total).astype(jnp.bfloat16)
        for copy in lse_copies:
            copy.wait_send()


def start_noise(noise_hbm, noise_wide, noise_sem):
    chunk = noise_wide.shape[1] // 4
    copies = []
    for k in range(4):
        columns = pl.ds(k * chunk, chunk)
        copy = pltpu.make_async_copy(
            noise_hbm.at[:, columns], noise_wide.at[:, columns], noise_sem.at[k]
        )
        copy.start()
        copies.append(copy)
    return copies


def round_noise(copies, noise_wide, noise_rows):
    noise_count, part_width = noise_rows.shape[1:]
    per_chunk = noise_rows.shape[0] // 4
    noise_norm = jnp.zeros((noise_count, 1), jnp.float32)
    for k in range(4):
        copies[k].wait()
        for s in range(per_chunk):
            q = k * per_chunk + s
            block = noise_wide[:, q * part_width : (q + 1) * part_width].astype(jnp.bfloat16)
            noise_rows[q] = block
            wide = block.astype(jnp.float32)
            noise_norm += jnp.sum(wide * wide, axis=1, keepdims=True)
    return noise_norm


def marked_live(slots_ref):
    marks = jnp.concatenate(
        [
            lax.dot_general(
                jnp.ones((8, LANES), jnp.bfloat16), slots_ref[0, t], CONTRACT_LAST,
                preferred_element_type=jnp.float32,
            )[0:1]
            for t in range(slots_ref.shape[1])
        ],
        axis=0,
    )
    return (marks < 0.5 * LANES * EMPTY).astype(jnp.float32)


def all_slots_kernel(width, slots_ref, noise_hbm, rows, weights, noise_wide, noise_sem, *scratch):
    noise_rows, live = scratch[1], scratch[3]
    members = SIDE * SIDE
    me = lax.axis_index("member")
    noise_copies = start_noise(noise_hbm, noise_wide, noise_sem)
    barrier = pltpu.get_barrier_semaphore()
    for k in range(1, members):
        pl.semaphore_signal(
            barrier, inc=1, device_id={"member": (me + k) % members}, device_id_type=MESH
        )
    live[...] = marked_live(slots_ref)
    for part in range(2):
        for t in range(members):
            block = slots_ref[part, t].astype(jnp.float32)
            block = jnp.where(block < 0.5 * EMPTY, block, 0.0)
            rows[me, part, t * ROWS_DEV : (t + 1) * ROWS_DEV, :] = block.astype(jnp.bfloat16)
    pl.semaphore_wait(barrier, members - 1)
    solve(
        width, rows.shape[2], False, lambda part: None, lambda: None,
        lambda: round_noise(noise_copies, noise_wide, noise_rows), rows, weights, scratch,
    )


def live_rows_kernel(
    width,
    sent,
    dest_hbm,
    loaded_hbm,
    noise_hbm,
    rows,
    weights,
    slots_ref,
    over_ref,
    dest_ref,
    loaded_ref,
    packed,
    landed,
    tally_bucket,
    tally_member,
    load_sem,
    bucket_send,
    bucket_recv,
    member_send,
    member_recv,
    tally_send,
    tally_recv,
    position,
    choose,
    noise_wide,
    noise_sem,
    *scratch,
):
    noise_rows, live = scratch[1], scratch[3]
    groups, members = BUCKETS, SIDE * SIDE
    loaded = loaded_ref.shape[0]
    capacity = rows.shape[2]
    tiles = capacity // LANES
    part_width = width // members
    block = ROWS_DEV // groups
    my_bucket, me = lax.axis_index("bucket"), lax.axis_index("member")
    bucket_peers = [(my_bucket + k) % groups for k in range(groups)]
    member_peers = [(me + k) % members for k in range(members)]

    dest_copy = pltpu.make_async_copy(dest_hbm, dest_ref, load_sem.at[0])
    dest_copy.start()
    load_copy = pltpu.make_async_copy(loaded_hbm, loaded_ref, load_sem.at[1])
    load_copy.start()
    noise_copies = start_noise(noise_hbm, noise_wide, noise_sem)
    barrier = pltpu.get_barrier_semaphore()
    for peer in bucket_peers[1:]:
        pl.semaphore_signal(barrier, inc=1, device_id={"bucket": peer}, device_id_type=MESH)
    for peer in member_peers[1:]:
        pl.semaphore_signal(barrier, inc=1, device_id={"member": peer}, device_id_type=MESH)

    dest_copy.wait()
    dest = dest_ref[...]
    hits = (lax.broadcasted_iota(jnp.int32, (groups, loaded), 0) == dest).astype(jnp.float32)
    up_to = (
        lax.broadcasted_iota(jnp.int32, (loaded, loaded), 0)
        <= lax.broadcasted_iota(jnp.int32, (loaded, loaded), 1)
    ).astype(jnp.bfloat16)
    ranks = jnp.dot(hits.astype(jnp.bfloat16), up_to, preferred_element_type=jnp.float32)
    place = jnp.sum(hits * (ranks - 1.0), axis=0, keepdims=True).astype(jnp.int32) + dest * block
    pick = lax.broadcasted_iota(jnp.int32, (ROWS_DEV, loaded), 0) == place
    pick = pick.astype(jnp.float32)
    fill = EMPTY * (1.0 - jnp.sum(pick, axis=1, keepdims=True))
    pick = pick.astype(jnp.bfloat16)
    tally_bucket[my_bucket] = jnp.broadcast_to(
        jnp.sum(hits, axis=1, keepdims=True), (groups, LANES)
    )
    load_copy.wait()

    def pack(k):
        start = pl.multiple_of(member_peers[k] * part_width, part_width)
        panel = loaded_ref[:, pl.ds(start, part_width)].astype(jnp.bfloat16)
        sorted_panel = jnp.dot(pick, panel, preferred_element_type=jnp.float32) + fill
        sorted_panel = sorted_panel.astype(jnp.bfloat16)
        for part in range(2):
            packed[part, k] = sorted_panel[:, part * LANES : (part + 1) * LANES]

    def block_of(bucket):
        return pl.ds(pl.multiple_of(bucket * block, block), block)

    def to_bucket(stage, k, source, target):
        copy = pltpu.make_async_remote_copy(
            src_ref=source.at[:, block_of(bucket_peers[k])],
            dst_ref=target.at[:, block_of(my_bucket)],
            send_sem=bucket_send.at[stage, k],
            recv_sem=bucket_recv.at[stage, k],
            device_id={"bucket": bucket_peers[k]},
            device_id_type=MESH,
        )
        copy.start()
        return copy

    def to_member(stage, k, source, target):
        copy = pltpu.make_async_remote_copy(
            src_ref=source,
            dst_ref=target,
            send_sem=member_send.at[stage, k],
            recv_sem=member_recv.at[stage, k],
            device_id={"member": member_peers[k]},
            device_id_type=MESH,
        )
        copy.start()
        return copy

    def tell(stage, k, source, target, axis, peer):
        copy = pltpu.make_async_remote_copy(
            src_ref=source,
            dst_ref=target,
            send_sem=tally_send.at[stage, k],
            recv_sem=tally_recv.at[stage, k],
            device_id={axis: peer},
            device_id_type=MESH,
        )
        copy.start()
        return copy

    for k in range(members):
        pack(k)
    pl.semaphore_wait(barrier, groups + members - 2)
    my_tally = tally_bucket.at[my_bucket]
    bucket_tally = [
        tell(0, k, my_tally, my_tally, "bucket", bucket_peers[k]) for k in range(1, groups)
    ]
    first_bucket, first_member = [], []
    for k in range(1, members):
        if k < groups:
            first_bucket.append(to_bucket(0, k, packed.at[0], landed.at[0]))
        first_member.append(to_member(0, k, packed.at[1, k], landed.at[1, me]))
    landed[0, :, block_of(my_bucket), :] = packed[0, :, block_of(my_bucket), :]
    landed[1, me] = packed[1, 0]

    for copy in bucket_tally:
        copy.wait_recv()
    total = jnp.zeros((groups, LANES), jnp.float32)
    for b in range(groups):
        tally_member[me, b : b + 1, :] = tally_bucket[b, pl.ds(my_bucket, 1), :]
        total += tally_bucket[b]
    tally_member[me, groups:, :] = total
    my_tallies = tally_member.at[me]
    member_tally = [
        tell(1, k, my_tallies, my_tallies, "member", member_peers[k]) for k in range(1, members)
    ]
    noise_norm = round_noise(noise_copies, noise_wide, noise_rows)
    if sent < capacity:
        blank = jnp.zeros((capacity - sent, LANES), jnp.bfloat16)
        for q in range(members):
            for part in range(2):
                rows[q, part, sent:capacity, :] = blank

    for copy in first_bucket:
        copy.wait_recv()
    second_member = [
        to_member(1, k, landed.at[0, k], slots_ref.at[0, me]) for k in range(1, members)
    ]
    slots_ref[0, me] = landed[0, 0]
    for copy in first_member:
        copy.wait_recv()
    second_bucket = [to_bucket(1, k, landed.at[1], slots_ref.at[1]) for k in range(1, groups)]
    slots_ref[1, :, block_of(my_bucket), :] = landed[1, :, block_of(my_bucket), :]
    def find_positions():
        for copy in member_tally:
            copy.wait_recv()
        lane = lax.broadcasted_iota(jnp.int32, (groups, LANES), 1)
        loader = lax.broadcasted_iota(jnp.int32, (groups, LANES), 0)
        of_loader = (lane // block == loader).astype(jnp.float32)
        filled = jnp.concatenate(
            [
                jnp.sum(of_loader * tally_member[m, :groups, :], axis=0, keepdims=True)
                for m in range(members)
            ],
            axis=0,
        )
        slot = lax.broadcasted_iota(jnp.int32, (members, LANES), 1) % block
        alive = (slot.astype(jnp.float32) < filled).astype(jnp.float32)
        before = (
            lax.broadcasted_iota(jnp.int32, (LANES, LANES), 0)
            <= lax.broadcasted_iota(jnp.int32, (LANES, LANES), 1)
        ).astype(jnp.bfloat16)
        inside = jnp.dot(alive.astype(jnp.bfloat16), before, preferred_element_type=jnp.float32)
        per_member = jnp.broadcast_to(inside[:, LANES - 1 : LANES], (members, LANES))
        earlier = (
            lax.broadcasted_iota(jnp.int32, (members, members), 0)
            > lax.broadcasted_iota(jnp.int32, (members, members), 1)
        ).astype(jnp.bfloat16)
        offset = jnp.dot(
            earlier, per_member.astype(jnp.bfloat16), preferred_element_type=jnp.float32
        )
        position[...] = jnp.where(alive > 0.5, inside + offset - 1.0, -1.0)
        held = jnp.sum(per_member, axis=0, keepdims=True)
        place = lax.broadcasted_iota(jnp.int32, (tiles, LANES), 0) * LANES
        place += lax.broadcasted_iota(jnp.int32, (tiles, LANES), 1)
        live[...] = (place.astype(jnp.float32) < held).astype(jnp.float32)

    find_positions()
    step = capacity // 9

    for start in range(0, capacity, step):
        target = lax.broadcasted_iota(jnp.int32, (step, LANES), 0) + start
        target = target.astype(jnp.float32)
        for t in range(start // LANES, members):
            choose[start : start + step, t * LANES : (t + 1) * LANES] = (
                target == position[t : t + 1, :]
            ).astype(jnp.bfloat16)

    def prepare(part):
        for copy in second_bucket if part else second_member:
            copy.wait_recv()
        slots = slots_ref[part].reshape(members * ROWS_DEV, LANES)
        for start in range(0, capacity, step):
            rows[me, part, start : start + step, :] = jnp.dot(
                choose[start : start + step, start:], slots[start:],
                preferred_element_type=jnp.float32,
            ).astype(jnp.bfloat16)

    def finish_count():
        total = tally_member[0, groups:, :]
        for m in range(1, members):
            total += tally_member[m, groups:, :]
        over_ref[0, 0] = (jnp.max(total) > sent).astype(jnp.int32)

    solve(width, sent, True, prepare, finish_count, lambda: noise_norm, rows, weights, scratch)
    for copy in (
        first_bucket + first_member + second_member + second_bucket + bucket_tally + member_tally
    ):
        copy.wait_send()


def solve_scratch(noise_count, capacity, width):
    members = SIDE * SIDE
    tiles = capacity // LANES
    dma = pltpu.SemaphoreType.DMA
    return [
        pltpu.VMEM((noise_count, width), jnp.float32),
        dma((4,)),
        pltpu.VMEM((noise_count, capacity), jnp.float32),
        pltpu.VMEM((members, noise_count, width // members), jnp.bfloat16),
        pltpu.VMEM((8, capacity), jnp.float32),
        pltpu.VMEM((tiles, LANES), jnp.float32),
        pltpu.VMEM((noise_count, LANES), jnp.float32),
        pltpu.VMEM((8, capacity), jnp.float32),
        pltpu.VMEM((ITERS, tiles, LANES), jnp.float32),
        pltpu.VMEM((ITERS, members, tiles, LANES), jnp.float32),
        dma((2, 2, 2)),
        dma((2, 2, 2)),
        dma((2, 2, 5, 2)),
        dma((2, 2, 5, 2)),
        dma((ITERS, members)),
        dma((ITERS, members)),
    ]


IN_VMEM = pl.BlockSpec(memory_space=pltpu.VMEM)
IN_HBM = pl.BlockSpec(memory_space=pltpu.HBM)


def in_hbm(array):
    return pltpu.with_memory_space_constraint(array, pltpu.HBM)


def pair_live_rows(dest_bucket, loader_rows, noise):
    members = SIDE * SIDE
    capacity = -(-FAST_ROWS // (3 * LANES)) * 3 * LANES
    loaded, width = loader_rows.shape
    noise_count = noise.shape[0]
    dma = pltpu.SemaphoreType.DMA
    return pl.pallas_call(
        functools.partial(live_rows_kernel, width, FAST_ROWS),
        out_shape=(
            jax.ShapeDtypeStruct((members, 2, capacity, LANES), jnp.bfloat16),
            jax.ShapeDtypeStruct((noise_count, capacity), jnp.bfloat16),
            jax.ShapeDtypeStruct((2, members, ROWS_DEV, LANES), jnp.bfloat16),
            jax.ShapeDtypeStruct((1, 1), jnp.int32),
        ),
        in_specs=[IN_HBM, IN_HBM, IN_HBM],
        out_specs=(IN_VMEM, IN_VMEM, IN_VMEM, pl.BlockSpec(memory_space=pltpu.SMEM)),
        scratch_shapes=[
            pltpu.VMEM((1, loaded), jnp.int32),
            pltpu.VMEM((loaded, width), jnp.float32),
            pltpu.VMEM((2, members, ROWS_DEV, LANES), jnp.bfloat16),
            pltpu.VMEM((2, members, ROWS_DEV, LANES), jnp.bfloat16),
            pltpu.VMEM((BUCKETS, BUCKETS, LANES), jnp.float32),
            pltpu.VMEM((members, 2 * BUCKETS, LANES), jnp.float32),
            dma((2,)),
            dma((2, BUCKETS)),
            dma((2, BUCKETS)),
            dma((2, members)),
            dma((2, members)),
            dma((2, members)),
            dma((2, members)),
            pltpu.VMEM((members, LANES), jnp.float32),
            pltpu.VMEM((capacity, members * ROWS_DEV), jnp.bfloat16),
            *solve_scratch(noise_count, capacity, width),
        ],
        compiler_params=pltpu.CompilerParams(
            collective_id=0, has_side_effects=True, vmem_limit_bytes=24 * 1024 * 1024
        ),
    )(*[in_hbm(array) for array in (dest_bucket.reshape(1, -1), loader_rows, noise)])


def pair_all_slots(slots, noise):
    members = SIDE * SIDE
    capacity = members * ROWS_DEV
    noise_count, width = noise.shape
    return pl.pallas_call(
        functools.partial(all_slots_kernel, width),
        out_shape=(
            jax.ShapeDtypeStruct((members, 2, capacity, LANES), jnp.bfloat16),
            jax.ShapeDtypeStruct((noise_count, capacity), jnp.bfloat16),
        ),
        in_specs=[IN_VMEM, IN_HBM],
        out_specs=(IN_VMEM, IN_VMEM),
        scratch_shapes=solve_scratch(noise_count, capacity, width),
        compiler_params=pltpu.CompilerParams(
            collective_id=1, has_side_effects=True, vmem_limit_bytes=14 * 1024 * 1024
        ),
    )(slots, noise)


def targets_kernel(rows_ref, weights_ref, out_hbm, made, sem):
    members = rows_ref.shape[0]
    part_width = 2 * LANES

    def out_copy(q):
        start = pl.multiple_of(q * part_width, part_width)
        return pltpu.make_async_copy(
            made.at[q], out_hbm.at[:, pl.ds(start, part_width)], sem.at[q]
        )

    @pl.loop(0, members, unroll=16)
    def _(q):
        panel = jnp.concatenate([rows_ref[q, 0], rows_ref[q, 1]], axis=1)
        made[q] = jnp.dot(weights_ref[...], panel, preferred_element_type=jnp.float32)
        out_copy(q).start()

    @pl.loop(0, members)
    def _(q):
        out_copy(q).wait()


def multiply(rows, weights):
    members = rows.shape[0]
    noise_count = weights.shape[0]
    width = members * 2 * LANES
    return pl.pallas_call(
        targets_kernel,
        out_shape=pltpu.HBM((noise_count, width), jnp.float32),
        in_specs=[IN_VMEM, IN_VMEM],
        out_specs=IN_HBM,
        scratch_shapes=[
            pltpu.VMEM((members, noise_count, 2 * LANES), jnp.float32),
            pltpu.SemaphoreType.DMA((members,)),
        ],
        compiler_params=pltpu.CompilerParams(vmem_limit_bytes=12 * 1024 * 1024),
    )(rows, weights)


def body(loader_rows, dest_bucket, dest_slot, noise):
    rows, weights, slots, over = pair_live_rows(dest_bucket, loader_rows, noise)
    targets = multiply(rows, weights)

    def with_all_slots(state):
        return jnp.zeros((), jnp.int32), multiply(*pair_all_slots(slots, noise))

    return lax.while_loop(lambda state: state[0] > 0, with_all_slots, (over[0, 0], targets))[1]


def solution(mesh):
    return jax.shard_map(
        body,
        mesh=mesh,
        in_specs=(
            P(("bucket", "member"), None),
            P(("bucket", "member")),
            P(("bucket", "member")),
            P(("bucket", "member"), None),
        ),
        out_specs=P(("bucket", "member"), None),
        check_vma=False,
    )
```

```python
import functools
import math

import jax
import jax.numpy as jnp
from jax import lax
from jax.experimental import pallas as pl
from jax.experimental.pallas import tpu as pltpu
from jax.sharding import PartitionSpec as P

ROWS_DEV = 128
ITERS = 4
SIDE = 4
BUCKETS = 8
FAST_ROWS = 1104
LANES = 128
EMPTY = 16384.0
MESH = pl.DeviceIdType.MESH
CONTRACT_LAST = (((1,), (1,)), ((), ()))


def hops(k):
    return sum(min(step, SIDE - step) for step in (k // SIDE, k % SIDE))


FAR_FIRST = sorted(range(1, SIDE * SIDE), key=lambda k: -hops(k))


def solve(width, sent, eager, prepare, extra, noise_norm_of, rows, weights, scratch):
    (cost, noise_rows, row_norm, live, col_shift, row_shift, lse_out, lse_in,
     first_send, first_recv, second_send, second_recv, lse_send, lse_recv) = scratch
    members = SIDE * SIDE
    capacity = rows.shape[2]
    noise_count = cost.shape[0]
    tiles = capacity // LANES
    scale = 1.0 / (width * (0.64 / math.sqrt(width)))
    me = lax.axis_index("member")
    my_z, my_x = me // SIDE, me % SIDE

    def member_at(part, first, second):
        along_x, along_z = (first, second) if part == 0 else (second, first)
        return ((my_z + along_z + SIDE) % SIDE) * SIDE + (my_x + along_x + SIDE) % SIDE

    def front(count):
        return -(-count // 32) * 16

    half = front(sent)
    units = [(0, 0, sent), (-1, 0, sent), (1, 0, sent), (2, 0, half), (2, half, sent - half)]
    ways = (1, -1)
    pending = {}

    def side(start, count, d):
        middle = front(count)
        return (start, middle) if d == 0 else (start + middle, count - middle)

    def send(label, part, owner, span, neighbour, sems):
        piece = rows.at[owner, part, pl.ds(*span)]
        copy = pltpu.make_async_remote_copy(
            src_ref=piece,
            dst_ref=piece,
            send_sem=sems[0],
            recv_sem=sems[1],
            device_id={"member": neighbour},
            device_id_type=MESH,
        )
        copy.start()
        pending[label] = copy

    def first_hop(part, d):
        sems = (first_send.at[part, 0, d], first_recv.at[part, 0, d])
        send(("f1", part, d), part, me, (0, sent), member_at(part, ways[d], 0), sems)

    def first_forward(part, d):
        sems = (first_send.at[part, 1, d], first_recv.at[part, 1, d])
        owner = member_at(part, -ways[d], 0)
        send(("f2", part, d), part, owner, side(0, sent, d), member_at(part, ways[d], 0), sems)

    def second_hop(part, u, d):
        first, start, count = units[u]
        sems = (second_send.at[part, 0, u, d], second_recv.at[part, 0, u, d])
        owner = me if u == 0 else member_at(part, first, 0)
        send(("g1", part, u, d), part, owner, (start, count), member_at(part, 0, ways[d]), sems)

    def second_forward(part, u, d):
        first, start, count = units[u]
        sems = (second_send.at[part, 1, u, d], second_recv.at[part, 1, u, d])
        owner = member_at(part, first, -ways[d])
        send(
            ("g2", part, u, d), part, owner, side(start, count, d), member_at(part, 0, ways[d]), sems
        )

    def arrive(label):
        pending[label].wait_recv()

    def add_slice(owner):
        if eager:
            add_panel(owner)

    def add_panel(owner):
        panel = jnp.concatenate([rows[owner, 0], rows[owner, 1]], axis=1)
        cost[...] += lax.dot_general(
            noise_rows[owner], panel, CONTRACT_LAST, preferred_element_type=jnp.float32
        )
        wide = panel.astype(jnp.float32)
        square = wide * wide
        high = square.astype(jnp.bfloat16)
        low = (square - high.astype(jnp.float32)).astype(jnp.bfloat16)
        ones = jnp.ones((8, panel.shape[1]), jnp.bfloat16)
        row_norm[...] += lax.dot_general(
            ones, high, CONTRACT_LAST, preferred_element_type=jnp.float32
        ) + lax.dot_general(ones, low, CONTRACT_LAST, preferred_element_type=jnp.float32)

    for part in range(2):
        prepare(part)
        for d in range(2):
            first_hop(part, d)
        for d in range(2):
            second_hop(part, 0, d)
    extra()
    cost[...] = jnp.zeros_like(cost)
    row_norm[...] = jnp.zeros_like(row_norm)
    noise_norm = noise_norm_of()
    add_slice(me)

    for part in range(2):
        for d in range(2):
            arrive(("f1", part, d))
            first_forward(part, d)
            u = 1 if d == 0 else 2
            for e in range(2):
                second_hop(part, u, e)
    for part in range(2):
        for d in range(2):
            arrive(("g1", part, 0, d))
            second_forward(part, 0, d)
    for step in ways:
        add_slice(member_at(0, step, 0))
        add_slice(member_at(0, 0, step))
    for d in range(2):
        for part in range(2):
            arrive(("f2", part, d))
            for e in range(2):
                second_hop(part, 3 + d, e)
    for u in (1, 2):
        for part in range(2):
            for d in range(2):
                arrive(("g1", part, u, d))
                second_forward(part, u, d)
    for step in ways:
        for other in ways:
            add_slice(member_at(0, step, other))
    for u in (3, 4):
        for part in range(2):
            for d in range(2):
                arrive(("g1", part, u, d))
                second_forward(part, u, d)
    for part in range(2):
        for d in range(2):
            arrive(("g2", part, 0, d))
    for part in range(2):
        add_slice(member_at(part, 2, 0))
    for u in (1, 2):
        for part in range(2):
            for d in range(2):
                arrive(("g2", part, u, d))
        for part in range(2):
            add_slice(member_at(part, units[u][0], 2))
    for u in (3, 4):
        for part in range(2):
            for d in range(2):
                arrive(("g2", part, u, d))
    add_slice(member_at(0, 2, 2))
    for copy in pending.values():
        copy.wait_send()

    if not eager:
        pl.loop(0, members)(add_panel)

    for t in range(tiles):
        lanes = slice(t * LANES, (t + 1) * LANES)
        cost[:, lanes] = (2.0 * cost[:, lanes] - row_norm[0:1, lanes] - noise_norm) * scale

    col_shift[...] = jnp.zeros_like(col_shift)
    row_chunk = 32
    for it in range(ITERS):
        for t in range(tiles):
            lanes = slice(t * LANES, (t + 1) * LANES)
            scores = cost[:, lanes] + col_shift[...]
            peak = jnp.max(scores, axis=0, keepdims=True)
            total = jnp.sum(jnp.exp(scores - peak), axis=0, keepdims=True)
            lse_out[it, t : t + 1, :] = peak + jnp.log(total)
        lse_copies = []
        for k in FAR_FIRST:
            copy = pltpu.make_async_remote_copy(
                src_ref=lse_out.at[it],
                dst_ref=lse_in.at[it, k],
                send_sem=lse_send.at[it, k],
                recv_sem=lse_recv.at[it, k],
                device_id={"member": member_at(0, k % SIDE, k // SIDE)},
                device_id_type=MESH,
            )
            copy.start()
            lse_copies.append(copy)
        for copy in lse_copies:
            copy.wait_recv()
        peak = lse_out[it]
        for k in range(1, members):
            peak = jnp.maximum(peak, lse_in[it, k])
        total = jnp.exp(lse_out[it] - peak)
        for k in range(1, members):
            total += jnp.exp(lse_in[it, k] - peak)
        shift = -(peak + jnp.log(total))
        for t in range(tiles):
            lanes = slice(t * LANES, (t + 1) * LANES)
            row_shift[0:1, lanes] = jnp.where(
                live[t : t + 1, :] > 0.5, shift[t : t + 1, :], -jnp.inf
            )
        for c in range(noise_count // row_chunk):
            span = slice(c * row_chunk, (c + 1) * row_chunk)
            scores = cost[span, :] + row_shift[0:1, :]
            peak = jnp.max(scores, axis=1, keepdims=True)
            exponent = jnp.exp(scores - peak)
            total = jnp.sum(exponent, axis=1, keepdims=True)
            if it < ITERS - 1:
                col_shift[span, :] = jnp.broadcast_to(-(peak + jnp.log(total)), (row_chunk, LANES))
            else:
                weights[span, :] = (exponent / total).astype(jnp.bfloat16)
        for copy in lse_copies:
            copy.wait_send()


def start_noise(noise_hbm, noise_wide, noise_sem):
    chunk = noise_wide.shape[1] // 4
    copies = []
    for k in range(4):
        columns = pl.ds(k * chunk, chunk)
        copy = pltpu.make_async_copy(
            noise_hbm.at[:, columns], noise_wide.at[:, columns], noise_sem.at[k]
        )
        copy.start()
        copies.append(copy)
    return copies


def round_noise(copies, noise_wide, noise_rows):
    noise_count, part_width = noise_rows.shape[1:]
    per_chunk = noise_rows.shape[0] // 4
    noise_norm = jnp.zeros((noise_count, 1), jnp.float32)
    for k in range(4):
        copies[k].wait()
        for s in range(per_chunk):
            q = k * per_chunk + s
            block = noise_wide[:, q * part_width : (q + 1) * part_width].astype(jnp.bfloat16)
            noise_rows[q] = block
            wide = block.astype(jnp.float32)
            noise_norm += jnp.sum(wide * wide, axis=1, keepdims=True)
    return noise_norm


def marked_live(slots_ref):
    marks = jnp.concatenate(
        [
            lax.dot_general(
                jnp.ones((8, LANES), jnp.bfloat16), slots_ref[0, t], CONTRACT_LAST,
                preferred_element_type=jnp.float32,
            )[0:1]
            for t in range(slots_ref.shape[1])
        ],
        axis=0,
    )
    return (marks < 0.5 * LANES * EMPTY).astype(jnp.float32)


def all_slots_kernel(width, slots_ref, noise_hbm, rows, weights, noise_wide, noise_sem, *scratch):
    noise_rows, live = scratch[1], scratch[3]
    members = SIDE * SIDE
    me = lax.axis_index("member")
    noise_copies = start_noise(noise_hbm, noise_wide, noise_sem)
    barrier = pltpu.get_barrier_semaphore()
    for k in range(1, members):
        pl.semaphore_signal(
            barrier, inc=1, device_id={"member": (me + k) % members}, device_id_type=MESH
        )
    live[...] = marked_live(slots_ref)
    for part in range(2):
        for t in range(members):
            block = slots_ref[part, t].astype(jnp.float32)
            block = jnp.where(block < 0.5 * EMPTY, block, 0.0)
            rows[me, part, t * ROWS_DEV : (t + 1) * ROWS_DEV, :] = block.astype(jnp.bfloat16)
    pl.semaphore_wait(barrier, members - 1)
    solve(
        width, rows.shape[2], False, lambda part: None, lambda: None,
        lambda: round_noise(noise_copies, noise_wide, noise_rows), rows, weights, scratch,
    )


def live_rows_kernel(
    width,
    sent,
    dest_hbm,
    loaded_hbm,
    noise_hbm,
    rows,
    weights,
    slots_ref,
    over_ref,
    dest_ref,
    loaded_ref,
    packed,
    landed,
    tally_bucket,
    tally_member,
    load_sem,
    bucket_send,
    bucket_recv,
    member_send,
    member_recv,
    tally_send,
    tally_recv,
    position,
    choose,
    noise_wide,
    noise_sem,
    *scratch,
):
    noise_rows, live = scratch[1], scratch[3]
    groups, members = BUCKETS, SIDE * SIDE
    loaded = loaded_ref.shape[0]
    capacity = rows.shape[2]
    tiles = capacity // LANES
    part_width = width // members
    block = ROWS_DEV // groups
    my_bucket, me = lax.axis_index("bucket"), lax.axis_index("member")
    bucket_peers = [(my_bucket + k) % groups for k in range(groups)]
    member_peers = [
        ((me // SIDE + k // SIDE) % SIDE) * SIDE + (me % SIDE + k % SIDE) % SIDE
        for k in range(members)
    ]

    dest_copy = pltpu.make_async_copy(dest_hbm, dest_ref, load_sem.at[0])
    dest_copy.start()
    load_copy = pltpu.make_async_copy(loaded_hbm, loaded_ref, load_sem.at[1])
    load_copy.start()
    noise_copies = start_noise(noise_hbm, noise_wide, noise_sem)
    barrier = pltpu.get_barrier_semaphore()
    for peer in bucket_peers[1:]:
        pl.semaphore_signal(barrier, inc=1, device_id={"bucket": peer}, device_id_type=MESH)
    for peer in member_peers[1:]:
        pl.semaphore_signal(barrier, inc=1, device_id={"member": peer}, device_id_type=MESH)

    dest_copy.wait()
    dest = dest_ref[...]
    hits = (lax.broadcasted_iota(jnp.int32, (groups, loaded), 0) == dest).astype(jnp.float32)
    up_to = (
        lax.broadcasted_iota(jnp.int32, (loaded, loaded), 0)
        <= lax.broadcasted_iota(jnp.int32, (loaded, loaded), 1)
    ).astype(jnp.bfloat16)
    ranks = jnp.dot(hits.astype(jnp.bfloat16), up_to, preferred_element_type=jnp.float32)
    place = jnp.sum(hits * (ranks - 1.0), axis=0, keepdims=True).astype(jnp.int32) + dest * block
    pick = lax.broadcasted_iota(jnp.int32, (ROWS_DEV, loaded), 0) == place
    pick = pick.astype(jnp.float32)
    fill = EMPTY * (1.0 - jnp.sum(pick, axis=1, keepdims=True))
    pick = pick.astype(jnp.bfloat16)
    tally_bucket[my_bucket] = jnp.broadcast_to(
        jnp.sum(hits, axis=1, keepdims=True), (groups, LANES)
    )
    load_copy.wait()

    def pack(k):
        start = pl.multiple_of(member_peers[k] * part_width, part_width)
        panel = loaded_ref[:, pl.ds(start, part_width)].astype(jnp.bfloat16)
        sorted_panel = jnp.dot(pick, panel, preferred_element_type=jnp.float32) + fill
        sorted_panel = sorted_panel.astype(jnp.bfloat16)
        for part in range(2):
            packed[part, k] = sorted_panel[:, part * LANES : (part + 1) * LANES]

    def block_of(bucket):
        return pl.ds(pl.multiple_of(bucket * block, block), block)

    def to_bucket(stage, k, source, target):
        copy = pltpu.make_async_remote_copy(
            src_ref=source.at[:, block_of(bucket_peers[k])],
            dst_ref=target.at[:, block_of(my_bucket)],
            send_sem=bucket_send.at[stage, k],
            recv_sem=bucket_recv.at[stage, k],
            device_id={"bucket": bucket_peers[k]},
            device_id_type=MESH,
        )
        copy.start()
        return copy

    def to_member(stage, k, source, target):
        copy = pltpu.make_async_remote_copy(
            src_ref=source,
            dst_ref=target,
            send_sem=member_send.at[stage, k],
            recv_sem=member_recv.at[stage, k],
            device_id={"member": member_peers[k]},
            device_id_type=MESH,
        )
        copy.start()
        return copy

    def tell(stage, k, source, target, axis, peer):
        copy = pltpu.make_async_remote_copy(
            src_ref=source,
            dst_ref=target,
            send_sem=tally_send.at[stage, k],
            recv_sem=tally_recv.at[stage, k],
            device_id={axis: peer},
            device_id_type=MESH,
        )
        copy.start()
        return copy

    for k in range(members):
        pack(k)
    first_bucket, second_member = {}, []

    def send_quarter(c):
        quarter = pl.ds(SIDE * c, SIDE)
        for k in range(1, groups):
            first_bucket[c, k] = to_bucket(
                c, k, packed.at[0, quarter], landed.at[0, quarter]
            )

    def pass_quarter(c):
        for k in range(1, groups):
            first_bucket[c, k].wait_recv()
        for k in FAR_FIRST:
            if k // SIDE == c:
                second_member.append(to_member(1, k, landed.at[0, k], slots_ref.at[0, me]))
        if c == 0:
            slots_ref[0, me] = landed[0, 0]

    order = (2, 1, 3, 0)
    pl.semaphore_wait(barrier, groups + members - 2)
    my_tally = tally_bucket.at[my_bucket]
    bucket_tally = [
        tell(0, k, my_tally, my_tally, "bucket", bucket_peers[k]) for k in range(1, groups)
    ]
    send_quarter(order[0])
    first_member = [to_member(0, k, packed.at[1, k], landed.at[1, me]) for k in FAR_FIRST]
    send_quarter(order[1])
    landed[0, :, block_of(my_bucket), :] = packed[0, :, block_of(my_bucket), :]
    landed[1, me] = packed[1, 0]

    for copy in bucket_tally:
        copy.wait_recv()
    total = jnp.zeros((groups, LANES), jnp.float32)
    for b in range(groups):
        tally_member[me, b : b + 1, :] = tally_bucket[b, pl.ds(my_bucket, 1), :]
        total += tally_bucket[b]
    tally_member[me, groups:, :] = total
    my_tallies = tally_member.at[me]
    member_tally = [
        tell(1, k, my_tallies, my_tallies, "member", member_peers[k]) for k in FAR_FIRST
    ]
    for i in range(2):
        for k in range(1, groups):
            first_bucket[order[i], k].wait_send()
        send_quarter(order[i + 2])
        pass_quarter(order[i])
    pass_quarter(order[2])
    pass_quarter(order[3])
    for copy in first_member:
        copy.wait_recv()
    second_bucket = [to_bucket(4, k, landed.at[1], slots_ref.at[1]) for k in range(1, groups)]
    slots_ref[1, :, block_of(my_bucket), :] = landed[1, :, block_of(my_bucket), :]

    noise_norm = round_noise(noise_copies, noise_wide, noise_rows)
    if sent < capacity:
        blank = jnp.zeros((capacity - sent, LANES), jnp.bfloat16)
        for q in range(members):
            for part in range(2):
                rows[q, part, sent:capacity, :] = blank

    def find_positions():
        for copy in member_tally:
            copy.wait_recv()
        lane = lax.broadcasted_iota(jnp.int32, (groups, LANES), 1)
        loader = lax.broadcasted_iota(jnp.int32, (groups, LANES), 0)
        of_loader = (lane // block == loader).astype(jnp.float32)
        filled = jnp.concatenate(
            [
                jnp.sum(of_loader * tally_member[m, :groups, :], axis=0, keepdims=True)
                for m in range(members)
            ],
            axis=0,
        )
        slot = lax.broadcasted_iota(jnp.int32, (members, LANES), 1) % block
        alive = (slot.astype(jnp.float32) < filled).astype(jnp.float32)
        before = (
            lax.broadcasted_iota(jnp.int32, (LANES, LANES), 0)
            <= lax.broadcasted_iota(jnp.int32, (LANES, LANES), 1)
        ).astype(jnp.bfloat16)
        inside = jnp.dot(alive.astype(jnp.bfloat16), before, preferred_element_type=jnp.float32)
        per_member = jnp.broadcast_to(inside[:, LANES - 1 : LANES], (members, LANES))
        earlier = (
            lax.broadcasted_iota(jnp.int32, (members, members), 0)
            > lax.broadcasted_iota(jnp.int32, (members, members), 1)
        ).astype(jnp.bfloat16)
        offset = jnp.dot(
            earlier, per_member.astype(jnp.bfloat16), preferred_element_type=jnp.float32
        )
        position[...] = jnp.where(alive > 0.5, inside + offset - 1.0, -1.0)
        held = jnp.sum(per_member, axis=0, keepdims=True)
        place = lax.broadcasted_iota(jnp.int32, (tiles, LANES), 0) * LANES
        place += lax.broadcasted_iota(jnp.int32, (tiles, LANES), 1)
        live[...] = (place.astype(jnp.float32) < held).astype(jnp.float32)

    find_positions()
    step = capacity // 9

    for start in range(0, capacity, step):
        target = lax.broadcasted_iota(jnp.int32, (step, LANES), 0) + start
        target = target.astype(jnp.float32)
        for t in range(start // LANES, members):
            choose[start : start + step, t * LANES : (t + 1) * LANES] = (
                target == position[t : t + 1, :]
            ).astype(jnp.bfloat16)

    def prepare(part):
        for copy in second_bucket if part else second_member:
            copy.wait_recv()
        slots = slots_ref[part].reshape(members * ROWS_DEV, LANES)
        for start in range(0, capacity, step):
            rows[me, part, start : start + step, :] = jnp.dot(
                choose[start : start + step, start:], slots[start:],
                preferred_element_type=jnp.float32,
            ).astype(jnp.bfloat16)

    def finish_count():
        total = tally_member[0, groups:, :]
        for m in range(1, members):
            total += tally_member[m, groups:, :]
        over_ref[0, 0] = (jnp.max(total) > sent).astype(jnp.int32)

    solve(width, sent, True, prepare, finish_count, lambda: noise_norm, rows, weights, scratch)
    for copy in (
        [first_bucket[c, k] for c in order[2:] for k in range(1, groups)]
        + first_member + second_member + second_bucket + bucket_tally + member_tally
    ):
        copy.wait_send()


def solve_scratch(noise_count, capacity, width):
    members = SIDE * SIDE
    tiles = capacity // LANES
    dma = pltpu.SemaphoreType.DMA
    return [
        pltpu.VMEM((noise_count, width), jnp.float32),
        dma((4,)),
        pltpu.VMEM((noise_count, capacity), jnp.float32),
        pltpu.VMEM((members, noise_count, width // members), jnp.bfloat16),
        pltpu.VMEM((8, capacity), jnp.float32),
        pltpu.VMEM((tiles, LANES), jnp.float32),
        pltpu.VMEM((noise_count, LANES), jnp.float32),
        pltpu.VMEM((8, capacity), jnp.float32),
        pltpu.VMEM((ITERS, tiles, LANES), jnp.float32),
        pltpu.VMEM((ITERS, members, tiles, LANES), jnp.float32),
        dma((2, 2, 2)),
        dma((2, 2, 2)),
        dma((2, 2, 5, 2)),
        dma((2, 2, 5, 2)),
        dma((ITERS, members)),
        dma((ITERS, members)),
    ]


IN_VMEM = pl.BlockSpec(memory_space=pltpu.VMEM)
IN_HBM = pl.BlockSpec(memory_space=pltpu.HBM)


def in_hbm(array):
    return pltpu.with_memory_space_constraint(array, pltpu.HBM)


def pair_live_rows(dest_bucket, loader_rows, noise):
    members = SIDE * SIDE
    capacity = -(-FAST_ROWS // (3 * LANES)) * 3 * LANES
    loaded, width = loader_rows.shape
    noise_count = noise.shape[0]
    dma = pltpu.SemaphoreType.DMA
    return pl.pallas_call(
        functools.partial(live_rows_kernel, width, FAST_ROWS),
        out_shape=(
            jax.ShapeDtypeStruct((members, 2, capacity, LANES), jnp.bfloat16),
            jax.ShapeDtypeStruct((noise_count, capacity), jnp.bfloat16),
            jax.ShapeDtypeStruct((2, members, ROWS_DEV, LANES), jnp.bfloat16),
            jax.ShapeDtypeStruct((1, 1), jnp.int32),
        ),
        in_specs=[IN_HBM, IN_HBM, IN_HBM],
        out_specs=(IN_VMEM, IN_VMEM, IN_VMEM, pl.BlockSpec(memory_space=pltpu.SMEM)),
        scratch_shapes=[
            pltpu.VMEM((1, loaded), jnp.int32),
            pltpu.VMEM((loaded, width), jnp.float32),
            pltpu.VMEM((2, members, ROWS_DEV, LANES), jnp.bfloat16),
            pltpu.VMEM((2, members, ROWS_DEV, LANES), jnp.bfloat16),
            pltpu.VMEM((BUCKETS, BUCKETS, LANES), jnp.float32),
            pltpu.VMEM((members, 2 * BUCKETS, LANES), jnp.float32),
            dma((2,)),
            dma((5, BUCKETS)),
            dma((5, BUCKETS)),
            dma((2, members)),
            dma((2, members)),
            dma((2, members)),
            dma((2, members)),
            pltpu.VMEM((members, LANES), jnp.float32),
            pltpu.VMEM((capacity, members * ROWS_DEV), jnp.bfloat16),
            *solve_scratch(noise_count, capacity, width),
        ],
        compiler_params=pltpu.CompilerParams(
            collective_id=0, has_side_effects=True, vmem_limit_bytes=24 * 1024 * 1024
        ),
    )(*[in_hbm(array) for array in (dest_bucket.reshape(1, -1), loader_rows, noise)])


def pair_all_slots(slots, noise):
    members = SIDE * SIDE
    capacity = members * ROWS_DEV
    noise_count, width = noise.shape
    return pl.pallas_call(
        functools.partial(all_slots_kernel, width),
        out_shape=(
            jax.ShapeDtypeStruct((members, 2, capacity, LANES), jnp.bfloat16),
            jax.ShapeDtypeStruct((noise_count, capacity), jnp.bfloat16),
        ),
        in_specs=[IN_VMEM, IN_HBM],
        out_specs=(IN_VMEM, IN_VMEM),
        scratch_shapes=solve_scratch(noise_count, capacity, width),
        compiler_params=pltpu.CompilerParams(
            collective_id=1, has_side_effects=True, vmem_limit_bytes=14 * 1024 * 1024
        ),
    )(slots, noise)


def targets_kernel(rows_ref, weights_ref, out_hbm, made, sem):
    members = rows_ref.shape[0]
    part_width = 2 * LANES

    def out_copy(q):
        start = pl.multiple_of(q * part_width, part_width)
        return pltpu.make_async_copy(
            made.at[q], out_hbm.at[:, pl.ds(start, part_width)], sem.at[q]
        )

    @pl.loop(0, members, unroll=16)
    def _(q):
        panel = jnp.concatenate([rows_ref[q, 0], rows_ref[q, 1]], axis=1)
        made[q] = jnp.dot(weights_ref[...], panel, preferred_element_type=jnp.float32)
        out_copy(q).start()

    @pl.loop(0, members)
    def _(q):
        out_copy(q).wait()


def multiply(rows, weights):
    members = rows.shape[0]
    noise_count = weights.shape[0]
    width = members * 2 * LANES
    return pl.pallas_call(
        targets_kernel,
        out_shape=pltpu.HBM((noise_count, width), jnp.float32),
        in_specs=[IN_VMEM, IN_VMEM],
        out_specs=IN_HBM,
        scratch_shapes=[
            pltpu.VMEM((members, noise_count, 2 * LANES), jnp.float32),
            pltpu.SemaphoreType.DMA((members,)),
        ],
        compiler_params=pltpu.CompilerParams(vmem_limit_bytes=12 * 1024 * 1024),
    )(rows, weights)


def body(loader_rows, dest_bucket, dest_slot, noise):
    rows, weights, slots, over = pair_live_rows(dest_bucket, loader_rows, noise)
    targets = multiply(rows, weights)

    def with_all_slots(state):
        return jnp.zeros((), jnp.int32), multiply(*pair_all_slots(slots, noise))

    return lax.while_loop(lambda state: state[0] > 0, with_all_slots, (over[0, 0], targets))[1]


def solution(mesh):
    return jax.shard_map(
        body,
        mesh=mesh,
        in_specs=(
            P(("bucket", "member"), None),
            P(("bucket", "member")),
            P(("bucket", "member")),
            P(("bucket", "member"), None),
        ),
        out_specs=P(("bucket", "member"), None),
        check_vma=False,
    )
```

```python
import functools
import math

import jax
import jax.numpy as jnp
from jax import lax
from jax.experimental import pallas as pl
from jax.experimental.pallas import tpu as pltpu
from jax.sharding import PartitionSpec as P

ROWS_DEV = 128
ITERS = 4
SIDE = 4
BUCKETS = 8
FAST_ROWS = 1104
LANES = 128
EMPTY = 16384.0
MESH = pl.DeviceIdType.MESH
CONTRACT_LAST = (((1,), (1,)), ((), ()))


def hops(k):
    return sum(min(step, SIDE - step) for step in (k // SIDE, k % SIDE))


FAR_FIRST = sorted(range(1, SIDE * SIDE), key=lambda k: -hops(k))


def solve(width, sent, eager, prepare, extra, noise_norm_of, rows, weights, scratch):
    (cost, noise_rows, row_norm, live, col_shift, row_shift, lse_out, lse_in,
     first_send, first_recv, second_send, second_recv, lse_send, lse_recv) = scratch
    members = SIDE * SIDE
    capacity = rows.shape[2]
    noise_count = cost.shape[0]
    tiles = capacity // LANES
    scale = 1.0 / (width * (0.64 / math.sqrt(width)))
    me = lax.axis_index("member")
    my_z, my_x = me // SIDE, me % SIDE

    def member_at(part, first, second):
        along_x, along_z = (first, second) if part == 0 else (second, first)
        return ((my_z + along_z + SIDE) % SIDE) * SIDE + (my_x + along_x + SIDE) % SIDE

    def front(count):
        return -(-count // 32) * 16

    half = front(sent)
    units = [(0, 0, sent), (-1, 0, sent), (1, 0, sent), (2, 0, half), (2, half, sent - half)]
    ways = (1, -1)
    pending = {}

    def side(start, count, d):
        middle = front(count)
        return (start, middle) if d == 0 else (start + middle, count - middle)

    def send(label, part, owner, span, neighbour, sems):
        piece = rows.at[owner, part, pl.ds(*span)]
        copy = pltpu.make_async_remote_copy(
            src_ref=piece,
            dst_ref=piece,
            send_sem=sems[0],
            recv_sem=sems[1],
            device_id={"member": neighbour},
            device_id_type=MESH,
        )
        copy.start()
        pending[label] = copy

    def first_hop(part, d):
        sems = (first_send.at[part, 0, d], first_recv.at[part, 0, d])
        send(("f1", part, d), part, me, (0, sent), member_at(part, ways[d], 0), sems)

    def first_forward(part, d):
        sems = (first_send.at[part, 1, d], first_recv.at[part, 1, d])
        owner = member_at(part, -ways[d], 0)
        send(("f2", part, d), part, owner, side(0, sent, d), member_at(part, ways[d], 0), sems)

    def second_hop(part, u, d):
        first, start, count = units[u]
        sems = (second_send.at[part, 0, u, d], second_recv.at[part, 0, u, d])
        owner = me if u == 0 else member_at(part, first, 0)
        send(("g1", part, u, d), part, owner, (start, count), member_at(part, 0, ways[d]), sems)

    def second_forward(part, u, d):
        first, start, count = units[u]
        sems = (second_send.at[part, 1, u, d], second_recv.at[part, 1, u, d])
        owner = member_at(part, first, -ways[d])
        send(
            ("g2", part, u, d), part, owner, side(start, count, d), member_at(part, 0, ways[d]), sems
        )

    def arrive(label):
        pending[label].wait_recv()

    def add_slice(owner):
        if eager:
            add_panel(owner)

    def add_panel(owner):
        panel = jnp.concatenate([rows[owner, 0], rows[owner, 1]], axis=1)
        cost[...] += lax.dot_general(
            noise_rows[owner], panel, CONTRACT_LAST, preferred_element_type=jnp.float32
        )
        wide = panel.astype(jnp.float32)
        square = wide * wide
        high = square.astype(jnp.bfloat16)
        low = (square - high.astype(jnp.float32)).astype(jnp.bfloat16)
        ones = jnp.ones((8, panel.shape[1]), jnp.bfloat16)
        row_norm[...] += lax.dot_general(
            ones, high, CONTRACT_LAST, preferred_element_type=jnp.float32
        ) + lax.dot_general(ones, low, CONTRACT_LAST, preferred_element_type=jnp.float32)

    for part in range(2):
        prepare(part)
        for d in range(2):
            first_hop(part, d)
        for d in range(2):
            second_hop(part, 0, d)
    extra()
    cost[...] = jnp.zeros_like(cost)
    row_norm[...] = jnp.zeros_like(row_norm)
    noise_norm = noise_norm_of()
    add_slice(me)

    for part in range(2):
        for d in range(2):
            arrive(("f1", part, d))
            first_forward(part, d)
            u = 1 if d == 0 else 2
            for e in range(2):
                second_hop(part, u, e)
    for part in range(2):
        for d in range(2):
            arrive(("g1", part, 0, d))
            second_forward(part, 0, d)
    for d in range(2):
        for part in range(2):
            arrive(("f2", part, d))
            for e in range(2):
                second_hop(part, 3 + d, e)
    for step in ways:
        add_slice(member_at(0, step, 0))
        add_slice(member_at(0, 0, step))
    for u in (1, 2):
        for part in range(2):
            for d in range(2):
                arrive(("g1", part, u, d))
                second_forward(part, u, d)
    for step in ways:
        for other in ways:
            add_slice(member_at(0, step, other))
    for u in (3, 4):
        for part in range(2):
            for d in range(2):
                arrive(("g1", part, u, d))
                second_forward(part, u, d)
    for part in range(2):
        for d in range(2):
            arrive(("g2", part, 0, d))
    for part in range(2):
        add_slice(member_at(part, 2, 0))
    for u in (1, 2):
        for part in range(2):
            for d in range(2):
                arrive(("g2", part, u, d))
        for part in range(2):
            add_slice(member_at(part, units[u][0], 2))
    for u in (3, 4):
        for part in range(2):
            for d in range(2):
                arrive(("g2", part, u, d))
    add_slice(member_at(0, 2, 2))
    for copy in pending.values():
        copy.wait_send()

    if not eager:
        pl.loop(0, members)(add_panel)

    row_chunk = 32
    for it in range(ITERS):
        for t in range(tiles):
            lanes = slice(t * LANES, (t + 1) * LANES)
            if it == 0:
                scores = (2.0 * cost[:, lanes] - row_norm[0:1, lanes] - noise_norm) * scale
                cost[:, lanes] = scores
            else:
                scores = cost[:, lanes] + col_shift[...]
            peak = jnp.max(scores, axis=0, keepdims=True)
            total = jnp.sum(jnp.exp(scores - peak), axis=0, keepdims=True)
            lse_out[it, t : t + 1, :] = peak + jnp.log(total)
        lse_copies = []
        for k in FAR_FIRST:
            copy = pltpu.make_async_remote_copy(
                src_ref=lse_out.at[it],
                dst_ref=lse_in.at[it, k],
                send_sem=lse_send.at[it, k],
                recv_sem=lse_recv.at[it, k],
                device_id={"member": member_at(0, k % SIDE, k // SIDE)},
                device_id_type=MESH,
            )
            copy.start()
            lse_copies.append(copy)
        for copy in lse_copies:
            copy.wait_recv()
        peak = lse_out[it]
        for k in range(1, members):
            peak = jnp.maximum(peak, lse_in[it, k])
        total = jnp.exp(lse_out[it] - peak)
        for k in range(1, members):
            total += jnp.exp(lse_in[it, k] - peak)
        shift = -(peak + jnp.log(total))
        for t in range(tiles):
            lanes = slice(t * LANES, (t + 1) * LANES)
            row_shift[0:1, lanes] = jnp.where(
                live[t : t + 1, :] > 0.5, shift[t : t + 1, :], -jnp.inf
            )
        for c in range(noise_count // row_chunk):
            span = slice(c * row_chunk, (c + 1) * row_chunk)
            scores = cost[span, :] + row_shift[0:1, :]
            peak = jnp.max(scores, axis=1, keepdims=True)
            exponent = jnp.exp(scores - peak)
            total = jnp.sum(exponent, axis=1, keepdims=True)
            if it < ITERS - 1:
                col_shift[span, :] = jnp.broadcast_to(-(peak + jnp.log(total)), (row_chunk, LANES))
            else:
                weights[span, :] = (exponent / total).astype(jnp.bfloat16)
        for copy in lse_copies:
            copy.wait_send()


def start_noise(noise_hbm, noise_wide, noise_sem):
    chunk = noise_wide.shape[1] // 4
    copies = []
    for k in range(4):
        columns = pl.ds(k * chunk, chunk)
        copy = pltpu.make_async_copy(
            noise_hbm.at[:, columns], noise_wide.at[:, columns], noise_sem.at[k]
        )
        copy.start()
        copies.append(copy)
    return copies


def round_noise(copies, noise_wide, noise_rows):
    noise_count, part_width = noise_rows.shape[1:]
    per_chunk = noise_rows.shape[0] // 4
    noise_norm = jnp.zeros((noise_count, 1), jnp.float32)
    for k in range(4):
        copies[k].wait()
        for s in range(per_chunk):
            q = k * per_chunk + s
            block = noise_wide[:, q * part_width : (q + 1) * part_width].astype(jnp.bfloat16)
            noise_rows[q] = block
            wide = block.astype(jnp.float32)
            noise_norm += jnp.sum(wide * wide, axis=1, keepdims=True)
    return noise_norm


def marked_live(slots_ref):
    marks = jnp.concatenate(
        [
            lax.dot_general(
                jnp.ones((8, LANES), jnp.bfloat16), slots_ref[0, t], CONTRACT_LAST,
                preferred_element_type=jnp.float32,
            )[0:1]
            for t in range(slots_ref.shape[1])
        ],
        axis=0,
    )
    return (marks < 0.5 * LANES * EMPTY).astype(jnp.float32)


def all_slots_kernel(width, slots_ref, noise_hbm, rows, weights, noise_wide, noise_sem, *scratch):
    noise_rows, live = scratch[1], scratch[3]
    members = SIDE * SIDE
    me = lax.axis_index("member")
    noise_copies = start_noise(noise_hbm, noise_wide, noise_sem)
    barrier = pltpu.get_barrier_semaphore()
    for k in range(1, members):
        pl.semaphore_signal(
            barrier, inc=1, device_id={"member": (me + k) % members}, device_id_type=MESH
        )
    live[...] = marked_live(slots_ref)
    for part in range(2):
        for t in range(members):
            block = slots_ref[part, t].astype(jnp.float32)
            block = jnp.where(block < 0.5 * EMPTY, block, 0.0)
            rows[me, part, t * ROWS_DEV : (t + 1) * ROWS_DEV, :] = block.astype(jnp.bfloat16)
    pl.semaphore_wait(barrier, members - 1)
    solve(
        width, rows.shape[2], False, lambda part: None, lambda: None,
        lambda: round_noise(noise_copies, noise_wide, noise_rows), rows, weights, scratch,
    )


def live_rows_kernel(
    width,
    sent,
    dest_hbm,
    loaded_hbm,
    noise_hbm,
    rows,
    weights,
    slots_ref,
    over_ref,
    dest_ref,
    loaded_ref,
    packed,
    landed,
    tally_bucket,
    tally_member,
    load_sem,
    bucket_send,
    bucket_recv,
    member_send,
    member_recv,
    tally_send,
    tally_recv,
    position,
    choose,
    noise_wide,
    noise_sem,
    *scratch,
):
    noise_rows, live = scratch[1], scratch[3]
    groups, members = BUCKETS, SIDE * SIDE
    loaded = loaded_ref.shape[0]
    capacity = rows.shape[2]
    tiles = capacity // LANES
    part_width = width // members
    block = ROWS_DEV // groups
    my_bucket, me = lax.axis_index("bucket"), lax.axis_index("member")
    bucket_peers = [(my_bucket + k) % groups for k in range(groups)]
    member_peers = [
        ((me // SIDE + k // SIDE) % SIDE) * SIDE + (me % SIDE + k % SIDE) % SIDE
        for k in range(members)
    ]

    barrier = pltpu.get_barrier_semaphore()
    for k in FAR_FIRST:
        pl.semaphore_signal(
            barrier, inc=1, device_id={"member": member_peers[k]}, device_id_type=MESH
        )
    for peer in bucket_peers[1:]:
        pl.semaphore_signal(barrier, inc=1, device_id={"bucket": peer}, device_id_type=MESH)

    dest_copy = pltpu.make_async_copy(dest_hbm, dest_ref, load_sem.at[0])
    dest_copy.start()
    load_copy = pltpu.make_async_copy(loaded_hbm, loaded_ref, load_sem.at[1])
    load_copy.start()
    noise_copies = start_noise(noise_hbm, noise_wide, noise_sem)
    dest_copy.wait()
    dest = dest_ref[...]
    hits = (lax.broadcasted_iota(jnp.int32, (groups, loaded), 0) == dest).astype(jnp.float32)
    up_to = (
        lax.broadcasted_iota(jnp.int32, (loaded, loaded), 0)
        <= lax.broadcasted_iota(jnp.int32, (loaded, loaded), 1)
    ).astype(jnp.bfloat16)
    ranks = jnp.dot(hits.astype(jnp.bfloat16), up_to, preferred_element_type=jnp.float32)
    place = jnp.sum(hits * (ranks - 1.0), axis=0, keepdims=True).astype(jnp.int32) + dest * block
    pick = lax.broadcasted_iota(jnp.int32, (ROWS_DEV, loaded), 0) == place
    pick = pick.astype(jnp.float32)
    fill = EMPTY * (1.0 - jnp.sum(pick, axis=1, keepdims=True))
    pick = pick.astype(jnp.bfloat16)
    tally_bucket[my_bucket] = jnp.broadcast_to(
        jnp.sum(hits, axis=1, keepdims=True), (groups, LANES)
    )
    load_copy.wait()

    def pack(k):
        start = pl.multiple_of(member_peers[k] * part_width, part_width)
        panel = loaded_ref[:, pl.ds(start, part_width)].astype(jnp.bfloat16)
        sorted_panel = jnp.dot(pick, panel, preferred_element_type=jnp.float32) + fill
        sorted_panel = sorted_panel.astype(jnp.bfloat16)
        for part in range(2):
            packed[part, k] = sorted_panel[:, part * LANES : (part + 1) * LANES]

    def block_of(bucket):
        return pl.ds(pl.multiple_of(bucket * block, block), block)

    def to_bucket(stage, k, source, target):
        copy = pltpu.make_async_remote_copy(
            src_ref=source.at[:, block_of(bucket_peers[k])],
            dst_ref=target.at[:, block_of(my_bucket)],
            send_sem=bucket_send.at[stage, k],
            recv_sem=bucket_recv.at[stage, k],
            device_id={"bucket": bucket_peers[k]},
            device_id_type=MESH,
        )
        copy.start()
        return copy

    def to_member(stage, k, source, target):
        copy = pltpu.make_async_remote_copy(
            src_ref=source,
            dst_ref=target,
            send_sem=member_send.at[stage, k],
            recv_sem=member_recv.at[stage, k],
            device_id={"member": member_peers[k]},
            device_id_type=MESH,
        )
        copy.start()
        return copy

    def tell(stage, k, source, target, axis, peer):
        copy = pltpu.make_async_remote_copy(
            src_ref=source,
            dst_ref=target,
            send_sem=tally_send.at[stage, k],
            recv_sem=tally_recv.at[stage, k],
            device_id={axis: peer},
            device_id_type=MESH,
        )
        copy.start()
        return copy

    for k in range(members):
        pack(k)
    first_bucket, second_member = {}, []

    def send_quarter(c):
        quarter = pl.ds(SIDE * c, SIDE)
        for k in range(1, groups):
            first_bucket[c, k] = to_bucket(
                c, k, packed.at[0, quarter], landed.at[0, quarter]
            )

    def pass_quarter(c):
        for k in range(1, groups):
            first_bucket[c, k].wait_recv()
        for k in FAR_FIRST:
            if k // SIDE == c:
                second_member.append(to_member(1, k, landed.at[0, k], slots_ref.at[0, me]))
        if c == 0:
            slots_ref[0, me] = landed[0, 0]

    order = (2, 1, 3, 0)
    pl.semaphore_wait(barrier, groups + members - 2)
    my_tally = tally_bucket.at[my_bucket]
    bucket_tally = [
        tell(0, k, my_tally, my_tally, "bucket", bucket_peers[k]) for k in range(1, groups)
    ]
    send_quarter(order[0])
    first_member = [to_member(0, k, packed.at[1, k], landed.at[1, me]) for k in FAR_FIRST]
    send_quarter(order[1])
    landed[0, :, block_of(my_bucket), :] = packed[0, :, block_of(my_bucket), :]
    landed[1, me] = packed[1, 0]

    for copy in bucket_tally:
        copy.wait_recv()
    total = jnp.zeros((groups, LANES), jnp.float32)
    for b in range(groups):
        tally_member[me, b : b + 1, :] = tally_bucket[b, pl.ds(my_bucket, 1), :]
        total += tally_bucket[b]
    tally_member[me, groups:, :] = total
    my_tallies = tally_member.at[me]
    member_tally = [
        tell(1, k, my_tallies, my_tallies, "member", member_peers[k]) for k in FAR_FIRST
    ]
    for i in range(2):
        for k in range(1, groups):
            first_bucket[order[i], k].wait_send()
        send_quarter(order[i + 2])
        pass_quarter(order[i])
    pass_quarter(order[2])
    pass_quarter(order[3])
    for copy in first_member:
        copy.wait_recv()
    second_bucket = [to_bucket(4, k, landed.at[1], slots_ref.at[1]) for k in range(1, groups)]
    slots_ref[1, :, block_of(my_bucket), :] = landed[1, :, block_of(my_bucket), :]

    noise_norm = round_noise(noise_copies, noise_wide, noise_rows)
    if sent < capacity:
        blank = jnp.zeros((capacity - sent, LANES), jnp.bfloat16)
        for q in range(members):
            for part in range(2):
                rows[q, part, sent:capacity, :] = blank

    def find_positions():
        for copy in member_tally:
            copy.wait_recv()
        lane = lax.broadcasted_iota(jnp.int32, (groups, LANES), 1)
        loader = lax.broadcasted_iota(jnp.int32, (groups, LANES), 0)
        of_loader = (lane // block == loader).astype(jnp.float32)
        filled = jnp.concatenate(
            [
                jnp.sum(of_loader * tally_member[m, :groups, :], axis=0, keepdims=True)
                for m in range(members)
            ],
            axis=0,
        )
        slot = lax.broadcasted_iota(jnp.int32, (members, LANES), 1) % block
        alive = (slot.astype(jnp.float32) < filled).astype(jnp.float32)
        before = (
            lax.broadcasted_iota(jnp.int32, (LANES, LANES), 0)
            <= lax.broadcasted_iota(jnp.int32, (LANES, LANES), 1)
        ).astype(jnp.bfloat16)
        inside = jnp.dot(alive.astype(jnp.bfloat16), before, preferred_element_type=jnp.float32)
        per_member = jnp.broadcast_to(inside[:, LANES - 1 : LANES], (members, LANES))
        earlier = (
            lax.broadcasted_iota(jnp.int32, (members, members), 0)
            > lax.broadcasted_iota(jnp.int32, (members, members), 1)
        ).astype(jnp.bfloat16)
        offset = jnp.dot(
            earlier, per_member.astype(jnp.bfloat16), preferred_element_type=jnp.float32
        )
        position[...] = jnp.where(alive > 0.5, inside + offset - 1.0, -1.0)
        held = jnp.sum(per_member, axis=0, keepdims=True)
        place = lax.broadcasted_iota(jnp.int32, (tiles, LANES), 0) * LANES
        place += lax.broadcasted_iota(jnp.int32, (tiles, LANES), 1)
        live[...] = (place.astype(jnp.float32) < held).astype(jnp.float32)

    find_positions()
    step = capacity // 9

    for start in range(0, capacity, step):
        target = lax.broadcasted_iota(jnp.int32, (step, LANES), 0) + start
        target = target.astype(jnp.float32)
        for t in range(start // LANES, members):
            choose[start : start + step, t * LANES : (t + 1) * LANES] = (
                target == position[t : t + 1, :]
            ).astype(jnp.bfloat16)

    def prepare(part):
        for copy in second_bucket if part else second_member:
            copy.wait_recv()
        slots = slots_ref[part].reshape(members * ROWS_DEV, LANES)
        for start in range(0, capacity, step):
            rows[me, part, start : start + step, :] = jnp.dot(
                choose[start : start + step, start:], slots[start:],
                preferred_element_type=jnp.float32,
            ).astype(jnp.bfloat16)

    def finish_count():
        total = tally_member[0, groups:, :]
        for m in range(1, members):
            total += tally_member[m, groups:, :]
        over_ref[0, 0] = (jnp.max(total) > sent).astype(jnp.int32)

    solve(width, sent, True, prepare, finish_count, lambda: noise_norm, rows, weights, scratch)
    for copy in (
        [first_bucket[c, k] for c in order[2:] for k in range(1, groups)]
        + first_member + second_member + second_bucket + bucket_tally + member_tally
    ):
        copy.wait_send()


def solve_scratch(noise_count, capacity, width):
    members = SIDE * SIDE
    tiles = capacity // LANES
    dma = pltpu.SemaphoreType.DMA
    return [
        pltpu.VMEM((noise_count, width), jnp.float32),
        dma((4,)),
        pltpu.VMEM((noise_count, capacity), jnp.float32),
        pltpu.VMEM((members, noise_count, width // members), jnp.bfloat16),
        pltpu.VMEM((8, capacity), jnp.float32),
        pltpu.VMEM((tiles, LANES), jnp.float32),
        pltpu.VMEM((noise_count, LANES), jnp.float32),
        pltpu.VMEM((8, capacity), jnp.float32),
        pltpu.VMEM((ITERS, tiles, LANES), jnp.float32),
        pltpu.VMEM((ITERS, members, tiles, LANES), jnp.float32),
        dma((2, 2, 2)),
        dma((2, 2, 2)),
        dma((2, 2, 5, 2)),
        dma((2, 2, 5, 2)),
        dma((ITERS, members)),
        dma((ITERS, members)),
    ]


IN_VMEM = pl.BlockSpec(memory_space=pltpu.VMEM)
IN_HBM = pl.BlockSpec(memory_space=pltpu.HBM)


def in_hbm(array):
    return pltpu.with_memory_space_constraint(array, pltpu.HBM)


def pair_live_rows(dest_bucket, loader_rows, noise):
    members = SIDE * SIDE
    capacity = -(-FAST_ROWS // (3 * LANES)) * 3 * LANES
    loaded, width = loader_rows.shape
    noise_count = noise.shape[0]
    dma = pltpu.SemaphoreType.DMA
    return pl.pallas_call(
        functools.partial(live_rows_kernel, width, FAST_ROWS),
        out_shape=(
            jax.ShapeDtypeStruct((members, 2, capacity, LANES), jnp.bfloat16),
            jax.ShapeDtypeStruct((noise_count, capacity), jnp.bfloat16),
            jax.ShapeDtypeStruct((2, members, ROWS_DEV, LANES), jnp.bfloat16),
            jax.ShapeDtypeStruct((1, 1), jnp.int32),
        ),
        in_specs=[IN_HBM, IN_HBM, IN_HBM],
        out_specs=(IN_VMEM, IN_VMEM, IN_VMEM, pl.BlockSpec(memory_space=pltpu.SMEM)),
        scratch_shapes=[
            pltpu.VMEM((1, loaded), jnp.int32),
            pltpu.VMEM((loaded, width), jnp.float32),
            pltpu.VMEM((2, members, ROWS_DEV, LANES), jnp.bfloat16),
            pltpu.VMEM((2, members, ROWS_DEV, LANES), jnp.bfloat16),
            pltpu.VMEM((BUCKETS, BUCKETS, LANES), jnp.float32),
            pltpu.VMEM((members, 2 * BUCKETS, LANES), jnp.float32),
            dma((2,)),
            dma((5, BUCKETS)),
            dma((5, BUCKETS)),
            dma((2, members)),
            dma((2, members)),
            dma((2, members)),
            dma((2, members)),
            pltpu.VMEM((members, LANES), jnp.float32),
            pltpu.VMEM((capacity, members * ROWS_DEV), jnp.bfloat16),
            *solve_scratch(noise_count, capacity, width),
        ],
        compiler_params=pltpu.CompilerParams(
            collective_id=0, has_side_effects=True, vmem_limit_bytes=24 * 1024 * 1024
        ),
    )(*[in_hbm(array) for array in (dest_bucket.reshape(1, -1), loader_rows, noise)])


def pair_all_slots(slots, noise):
    members = SIDE * SIDE
    capacity = members * ROWS_DEV
    noise_count, width = noise.shape
    return pl.pallas_call(
        functools.partial(all_slots_kernel, width),
        out_shape=(
            jax.ShapeDtypeStruct((members, 2, capacity, LANES), jnp.bfloat16),
            jax.ShapeDtypeStruct((noise_count, capacity), jnp.bfloat16),
        ),
        in_specs=[IN_VMEM, IN_HBM],
        out_specs=(IN_VMEM, IN_VMEM),
        scratch_shapes=solve_scratch(noise_count, capacity, width),
        compiler_params=pltpu.CompilerParams(
            collective_id=1, has_side_effects=True, vmem_limit_bytes=14 * 1024 * 1024
        ),
    )(slots, noise)


def targets_kernel(rows_ref, weights_ref, out_hbm, made, sem):
    members = rows_ref.shape[0]
    part_width = 2 * LANES

    def out_copy(q):
        start = pl.multiple_of(q * part_width, part_width)
        return pltpu.make_async_copy(
            made.at[q], out_hbm.at[:, pl.ds(start, part_width)], sem.at[q]
        )

    @pl.loop(0, members, unroll=16)
    def _(q):
        panel = jnp.concatenate([rows_ref[q, 0], rows_ref[q, 1]], axis=1)
        made[q] = jnp.dot(weights_ref[...], panel, preferred_element_type=jnp.float32)
        out_copy(q).start()

    @pl.loop(0, members)
    def _(q):
        out_copy(q).wait()


def multiply(rows, weights):
    members = rows.shape[0]
    noise_count = weights.shape[0]
    width = members * 2 * LANES
    return pl.pallas_call(
        targets_kernel,
        out_shape=pltpu.HBM((noise_count, width), jnp.float32),
        in_specs=[IN_VMEM, IN_VMEM],
        out_specs=IN_HBM,
        scratch_shapes=[
            pltpu.VMEM((members, noise_count, 2 * LANES), jnp.float32),
            pltpu.SemaphoreType.DMA((members,)),
        ],
        compiler_params=pltpu.CompilerParams(vmem_limit_bytes=12 * 1024 * 1024),
    )(rows, weights)


def body(loader_rows, dest_bucket, dest_slot, noise):
    rows, weights, slots, over = pair_live_rows(dest_bucket, loader_rows, noise)
    targets = multiply(rows, weights)

    def with_all_slots(state):
        return jnp.zeros((), jnp.int32), multiply(*pair_all_slots(slots, noise))

    return lax.while_loop(lambda state: state[0] > 0, with_all_slots, (over[0, 0], targets))[1]


def solution(mesh):
    return jax.shard_map(
        body,
        mesh=mesh,
        in_specs=(
            P(("bucket", "member"), None),
            P(("bucket", "member")),
            P(("bucket", "member")),
            P(("bucket", "member"), None),
        ),
        out_specs=P(("bucket", "member"), None),
        check_vma=False,
    )
```
